32 devices in a mesh: dp: 8 (over z, y), zero: 4 (over x, core).
Axes of the slice: x: 2, y: 2, z: 4, core: 2. Of those that a mesh axis runs over, the one named last changes fastest.
Arguments:
- tokens: bfloat16 [8, 512, 768], P('dp', 'zero'), may hold values from -6 to 6
- cotangent: bfloat16 [8, 512, 768], P('dp', 'zero'), may hold values from -6 to 6
- params: float32 [4, 8, 156720], P('zero', 'dp'), may hold values from -2 to 2
- first_moment: float32 [4, 8, 156720], P('zero', 'dp'), may hold values from -0.15625 to 0.15625
- second_moment: float32 [4, 8, 156720], P('zero', 'dp'), may hold values from 0.005 to 0.05
Outputs:
- output: bfloat16 [8, 512, 768], P('dp', 'zero')
- grad_tokens: float32 [8, 512, 768], P('dp', 'zero')
- grad_params: float32 [4, 8, 156720], P('zero', 'dp')
- new_params: float32 [4, 8, 156720], P('zero', 'dp')
- new_first: float32 [4, 8, 156720], P('zero', 'dp')
- new_second: float32 [4, 8, 156720], P('zero', 'dp')
The draws below stay inside these ranges and needn't reach their ends.
All inputs are finite; a program needn't handle non-finite values.
Results may differ from the reference program's by a relative error of at most 0.019.
Values may be sent and summed in bfloat16 or wider, within the bound.
A program may use at most 128 MiB of HBM per device.

```python
import math
import jax
import jax.numpy as jnp
from jax import lax

D = 768
FF = 1152
HEAD = 64
HALF_WIN = 64
LENGTH = 512
SEQS = 8
TOKENS = 4096
SHARD = 156720
STEP = 3
N_DP = 8
N_ZERO = 4


def pack_drawn(w_qkv, w_attn, w_input, w_output, gain_one, gain_two):
    quarter = D // N_ZERO
    ff_part = FF // N_ZERO
    qkv_s = w_qkv.reshape(3, N_ZERO, quarter, D).transpose(1, 0, 2, 3).reshape(N_ZERO, 3 * quarter * D)
    attn_s = w_attn.reshape(D, N_ZERO, quarter).transpose(1, 0, 2).reshape(N_ZERO, D * quarter)
    attn_part = jnp.concatenate([qkv_s, attn_s, gain_one.reshape(N_ZERO, quarter), gain_two.reshape(N_ZERO, quarter)], axis=1)
    in_s = w_input.reshape(2, N_ZERO, ff_part, D).transpose(1, 0, 2, 3).reshape(N_ZERO, 2 * ff_part * D)
    out_s = w_output.reshape(D, N_ZERO, ff_part).transpose(1, 0, 2).reshape(N_ZERO, D * ff_part)
    ffn_part = jnp.concatenate([in_s, out_s], axis=1)
    return jnp.concatenate([ffn_part.reshape(N_ZERO, N_DP, -1), attn_part.reshape(N_ZERO, N_DP, -1)], axis=2)


def draw_params(key, part):
    subkeys = jax.random.split(key, 6)
    attn_in = jax.random.truncated_normal(subkeys[0], -4.0, 4.0, (3 * D, D), jnp.float32) * D ** (-0.5)
    attn_out = jax.random.truncated_normal(subkeys[1], -4.0, 4.0, (D, D), jnp.float32) * (2.0 * HALF_WIN / D) ** 0.5
    w_lift = jax.random.truncated_normal(subkeys[2], -4.0, 4.0, (2 * FF, D), jnp.float32) * D ** (-0.5)
    w_lower = jax.random.truncated_normal(subkeys[3], -4.0, 4.0, (D, FF), jnp.float32) * FF ** (-0.5)
    gain_one = jax.random.uniform(subkeys[4], (D,), jnp.float32, 0.5, 1.5)
    gain_two = jax.random.uniform(subkeys[5], (D,), jnp.float32, 0.5, 1.5)
    packed = pack_drawn(attn_in, attn_out, w_lift, w_lower, gain_one, gain_two)
    return jnp.clip(packed, -2.0, 2.0)


def strengthened(array, rng, source, target, parts, factor):
    owner, partner = [(jnp.arange(array.shape[dim]) // (array.shape[dim] // parts)).reshape([-1 if axis == dim else 1 for axis in range(array.ndim)]) for dim in (source, target)]
    chosen = jax.random.permutation(rng, parts)[partner]
    strong = (owner == chosen) | (owner == (partner + parts // 2) % parts)
    return jnp.where(strong, factor * array, array)


def shard_levels(rng, dims, cuts, low, largest):
    factor_of = 1.0
    for dim, parts in cuts:
        steps = jax.random.uniform(jax.random.fold_in(jax.random.fold_in(rng, 6), dim), (parts,), jnp.float32, low / len(cuts), largest / len(cuts))
        factor_of = factor_of * jnp.repeat(jnp.exp(steps), dims[dim] // parts).reshape((-1,) + (1,) * (len(dims) - 1 - dim))
    return factor_of


def scatter_about(key, extent, scale, most, cuts=(), kind=jnp.bfloat16):
    values = scale * jax.random.normal(key, extent, jnp.float32)
    if cuts:
        values = values * shard_levels(key, extent, cuts, -0.22, 0.18)
    return jnp.clip(values, -most, most).astype(kind)


def bell_draw_with(stream_key, extent, deviation, most, pieces, heavy, held_as=jnp.bfloat16):
    array = deviation * jax.random.normal(stream_key, extent, jnp.float32)
    if pieces:
        array = array * shard_levels(stream_key, extent, pieces, -0.22, 0.18)
    return jnp.clip(strengthened(array, jax.random.fold_in(stream_key, 3), *heavy), -most, most).astype(held_as)


def setup_inputs(seed: int = 0) -> dict:
    seeds = jax.random.split(jax.random.key(seed), 6)
    return {
        "tokens": scatter_about(seeds[0], (SEQS, LENGTH, D), 1.0, 6.0, ((0, 8), (1, 4))),
        "cotangent": bell_draw_with(seeds[1], (SEQS, LENGTH, D), 1.0, 6.0, ((0, 8), (1, 4)), (0, 2, 8, 2.0)),
        "params": draw_params(jax.random.fold_in(seeds[5], 71), 0),
        "first_moment": scatter_about(seeds[3], (N_ZERO, N_DP, SHARD), 0.01, 0.15625, ((0, 4), (1, 8)), jnp.float32),
        "second_moment": jnp.clip(jnp.exp(math.log(0.05) - 2.3025851 * jax.random.uniform(seeds[4], (N_ZERO, N_DP, SHARD), jnp.float32) ** shard_levels(seeds[4], (N_ZERO, N_DP, SHARD), ((0, 4), (1, 8)), -0.2, 0.2)), 0.005, 0.05),
    }


norm_eps = 1e-05
beta_one = 0.9
beta_two = 0.98
adam_eps = 1e-06
rope_base = 10000.0
matrix_rate = 0.01
matrix_decay = 0.1
gain_rate = 0.1
masked_score = -1e+30

def rounded(values):
    return lax.optimization_barrier(values.astype(jnp.bfloat16))

def pack_layout(w_qkv, w_attn, w_input, w_output, gain_one, gain_two):
    quarter = D // N_ZERO
    ff_part = FF // N_ZERO
    qkv_s = w_qkv.reshape(3, N_ZERO, quarter, D).transpose(1, 0, 2, 3).reshape(N_ZERO, 3 * quarter * D)
    attn_s = w_attn.reshape(D, N_ZERO, quarter).transpose(1, 0, 2).reshape(N_ZERO, D * quarter)
    attn_part = jnp.concatenate([qkv_s, attn_s, gain_one.reshape(N_ZERO, quarter), gain_two.reshape(N_ZERO, quarter)], axis=1)
    in_s = w_input.reshape(2, N_ZERO, ff_part, D).transpose(1, 0, 2, 3).reshape(N_ZERO, 2 * ff_part * D)
    out_s = w_output.reshape(D, N_ZERO, ff_part).transpose(1, 0, 2).reshape(N_ZERO, D * ff_part)
    ffn_part = jnp.concatenate([in_s, out_s], axis=1)
    return jnp.concatenate([ffn_part.reshape(N_ZERO, N_DP, -1), attn_part.reshape(N_ZERO, N_DP, -1)], axis=2)

def unpack_layout(packed):
    quarter = D // N_ZERO
    ff_part = FF // N_ZERO
    ffn_width = 3 * D * FF // N_ZERO // N_DP
    ffn_part = packed[:, :, :ffn_width].reshape(N_ZERO, -1)
    attn_part = packed[:, :, ffn_width:].reshape(N_ZERO, -1)
    first_end = 3 * quarter * D
    second_end = first_end + D * quarter
    w_qkv = attn_part[:, :first_end].reshape(N_ZERO, 3, quarter, D).transpose(1, 0, 2, 3).reshape(3 * D, D)
    w_attn = attn_part[:, first_end:second_end].reshape(N_ZERO, D, quarter).transpose(1, 0, 2).reshape(D, D)
    gain_one = attn_part[:, second_end:second_end + quarter].reshape(D)
    gain_two = attn_part[:, second_end + quarter:].reshape(D)
    lift_end = 2 * ff_part * D
    w_input = ffn_part[:, :lift_end].reshape(N_ZERO, 2, ff_part, D).transpose(1, 0, 2, 3).reshape(2 * FF, D)
    w_output = ffn_part[:, lift_end:].reshape(N_ZERO, D, ff_part).transpose(1, 0, 2).reshape(D, FF)
    return (w_qkv, w_attn, w_input, w_output, gain_one, gain_two)

def norm_forward(values):
    centred = values - lax.optimization_barrier(jnp.mean(values, axis=-1, keepdims=True))
    inverse = lax.rsqrt(lax.optimization_barrier(jnp.mean(centred * centred, axis=-1, keepdims=True)) + norm_eps)
    return (centred * inverse, inverse)

def norm_backward(grad_norm, gain_vec, normed, inverse):
    scaled = grad_norm * gain_vec
    return inverse * (scaled - lax.optimization_barrier(jnp.mean(scaled, axis=-1, keepdims=True)) - normed * lax.optimization_barrier(jnp.mean(scaled * normed, axis=-1, keepdims=True)))

def rotary_tables():
    position = jnp.arange(LENGTH, dtype=jnp.float32)
    exponent = jnp.arange(HEAD // 2, dtype=jnp.float32) * (2.0 / HEAD)
    inv_freq = jnp.exp(-math.log(rope_base) * exponent)
    phases = position[:, None] * inv_freq[None, :]
    cosine = jnp.concatenate([jnp.cos(phases), jnp.cos(phases)], axis=-1)[:, None, :]
    sine_table = jnp.concatenate([jnp.sin(phases), jnp.sin(phases)], axis=-1)[:, None, :]
    return (cosine, sine_table)

def rotate_half(values):
    middle = values.shape[-1] // 2
    return jnp.concatenate([-values[..., middle:], values[..., :middle]], axis=-1)

def rotate_back(values):
    middle = values.shape[-1] // 2
    return jnp.concatenate([values[..., middle:], -values[..., :middle]], axis=-1)

def gelu_parts(values):
    cdf_part = 0.5 * (1.0 + jax.scipy.special.erf(values * (1.0 / math.sqrt(2.0))))
    pdf_part = jnp.exp(-0.5 * values * values) * (1.0 / math.sqrt(2.0 * math.pi))
    return (values * cdf_part, cdf_part + values * pdf_part)

def slice_sum(left, right):
    terms = jnp.einsum('rzk,zkd->zrd', left.astype(jnp.float32), right.astype(jnp.float32))
    return lax.optimization_barrier(jnp.sum(rounded(terms).astype(jnp.float32), axis=0))

def group_pass(tokens, cotangent, weights, cosine, sine_table, allowed):
    w_qkv, w_attn, w_input, w_output, gain_one, gain_two = weights
    groups = tokens.shape[0]
    head_count = D // HEAD
    row_count = groups * LENGTH
    quarter = D // N_ZERO
    ff_part = FF // N_ZERO
    gain_one32 = gain_one.astype(jnp.float32)
    gain_two32 = gain_two.astype(jnp.float32)
    attn_right = w_attn.reshape(D, N_ZERO, quarter).transpose(1, 2, 0)
    output_right = w_output.reshape(D, N_ZERO, ff_part).transpose(1, 2, 0)
    input_right = w_input.reshape(2, N_ZERO, ff_part, D).transpose(1, 0, 2, 3).reshape(N_ZERO, 2 * ff_part, D)
    qkv_right = w_qkv.reshape(3, N_ZERO, quarter, D).transpose(1, 0, 2, 3).reshape(N_ZERO, 3 * quarter, D)
    inputs = tokens.astype(jnp.float32).reshape(row_count, D)
    normed_one, inverse_one = norm_forward(inputs)
    normal_one = rounded(normed_one * gain_one32)
    projected = jnp.dot(normal_one, w_qkv.T, preferred_element_type=jnp.float32)
    projected = projected.reshape(groups, LENGTH, 3, head_count, HEAD)
    queries = rounded(projected[:, :, 0] * cosine + rotate_half(projected[:, :, 0]) * sine_table)
    key_rows = rounded(projected[:, :, 1] * cosine + rotate_half(projected[:, :, 1]) * sine_table)
    value_rows = rounded(projected[:, :, 2])
    query32 = queries.astype(jnp.float32)
    key32 = key_rows.astype(jnp.float32)
    value32 = value_rows.astype(jnp.float32)
    scores = jnp.einsum('gqhe,gkhe->ghqk', query32, key32) * 0.125
    scores = jnp.where(allowed, scores, masked_score)
    row_max = lax.optimization_barrier(jnp.max(scores, axis=-1, keepdims=True))
    log_total = row_max + jnp.log(lax.optimization_barrier(jnp.sum(jnp.exp(scores - row_max), axis=-1, keepdims=True)))
    attn_probs = jnp.exp(scores - log_total)
    probs_b = rounded(attn_probs).astype(jnp.float32)
    context = rounded(jnp.einsum('ghqk,gkhe->gqhe', probs_b, value32))
    context_rows = context.reshape(row_count, D)
    hidden = inputs + slice_sum(context_rows.reshape(row_count, N_ZERO, quarter), attn_right)
    normed_two, inverse_two = norm_forward(hidden)
    normal_two = rounded(normed_two * gain_two32)
    lifted = jnp.dot(normal_two, w_input.T, preferred_element_type=jnp.float32)
    gate_act, gate_slope = gelu_parts(lifted[:, :FF])
    up_half = lifted[:, FF:]
    mixed = rounded(gate_act * up_half)
    output = hidden + slice_sum(mixed.reshape(row_count, N_ZERO, ff_part), output_right)
    grad_rows = cotangent.reshape(row_count, D)
    grad_output = jnp.dot(grad_rows.T, mixed, preferred_element_type=jnp.float32)
    grad_mixed = jnp.dot(grad_rows, w_output, preferred_element_type=jnp.float32)
    grad_lifted = rounded(jnp.concatenate([grad_mixed * up_half * gate_slope, grad_mixed * gate_act], axis=-1))
    grad_input = jnp.dot(grad_lifted.T, normal_two, preferred_element_type=jnp.float32)
    lifted_left = grad_lifted.reshape(row_count, 2, N_ZERO, ff_part).transpose(0, 2, 1, 3).reshape(row_count, N_ZERO, 2 * ff_part)
    grad_norm_two = slice_sum(lifted_left, input_right)
    grad_gain_two = lax.optimization_barrier(jnp.sum(grad_norm_two * normed_two, axis=0))
    grad_hidden = grad_rows.astype(jnp.float32) + norm_backward(grad_norm_two, gain_two32, normed_two, inverse_two)
    grad_hidden_b = rounded(grad_hidden)
    grad_attn = jnp.dot(grad_hidden_b.T, context_rows, preferred_element_type=jnp.float32)
    grad_context = rounded(jnp.dot(grad_hidden_b, w_attn, preferred_element_type=jnp.float32))
    grad_context32 = grad_context.astype(jnp.float32).reshape(groups, LENGTH, head_count, HEAD)
    grad_probs = jnp.einsum('gqhe,gkhe->ghqk', grad_context32, value32)
    row_term = lax.optimization_barrier(jnp.sum(grad_context32 * context.astype(jnp.float32), axis=-1))
    row_term = jnp.transpose(row_term, (0, 2, 1))[..., None]
    grad_scores = rounded(attn_probs * (grad_probs - row_term) * 0.125).astype(jnp.float32)
    grad_query = jnp.einsum('ghqk,gkhe->gqhe', grad_scores, key32)
    grad_key = jnp.einsum('ghqk,gqhe->gkhe', grad_scores, query32)
    grad_value = jnp.einsum('ghqk,gqhe->gkhe', probs_b, grad_context32)
    grad_query = grad_query * cosine + rotate_back(grad_query * sine_table)
    grad_key = grad_key * cosine + rotate_back(grad_key * sine_table)
    grad_packed = rounded(jnp.stack([grad_query, grad_key, grad_value], axis=2)).reshape(row_count, 3 * D)
    grad_qkv = jnp.dot(grad_packed.T, normal_one, preferred_element_type=jnp.float32)
    packed_left = grad_packed.reshape(row_count, 3, N_ZERO, quarter).transpose(0, 2, 1, 3).reshape(row_count, N_ZERO, 3 * quarter)
    grad_norm_one = slice_sum(packed_left, qkv_right)
    grad_gain_one = lax.optimization_barrier(jnp.sum(grad_norm_one * normed_one, axis=0))
    grad_inputs = grad_hidden + norm_backward(grad_norm_one, gain_one32, normed_one, inverse_one)
    grad_parts = (grad_qkv, grad_attn, grad_input, grad_output, grad_gain_one, grad_gain_two)
    return (output.astype(jnp.bfloat16).reshape(tokens.shape), grad_inputs.reshape(tokens.shape), grad_parts)

def reference(tokens, cotangent, params, first_moment, second_moment):
    weights = unpack_layout(rounded(params))
    cosine, sine_table = rotary_tables()
    places = jnp.arange(LENGTH, dtype=jnp.int32)
    allowed = jnp.abs(places[:, None] - places[None, :]) <= HALF_WIN
    group_size = 8
    group_steps = SEQS // group_size
    token_groups = tokens.reshape(group_steps, group_size, LENGTH, D)
    cot_groups = cotangent.reshape(group_steps, group_size, LENGTH, D)
    zero_parts = (jnp.zeros((3 * D, D), jnp.float32), jnp.zeros((D, D), jnp.float32), jnp.zeros((2 * FF, D), jnp.float32), jnp.zeros((D, FF), jnp.float32), jnp.zeros((D,), jnp.float32), jnp.zeros((D,), jnp.float32))

    def advance(grad_total, block_pair):
        output, grad_inputs, grad_parts = group_pass(block_pair[0], block_pair[1], weights, cosine, sine_table, allowed)
        summed = tuple((total + part for total, part in zip(grad_total, grad_parts)))
        return (summed, (output, grad_inputs))
    grad_total, (outputs, grad_inputs) = lax.scan(advance, zero_parts, (token_groups, cot_groups))
    grad_params = pack_layout(*grad_total) * float(TOKENS) ** (-0.5)
    new_first = beta_one * first_moment + (1.0 - beta_one) * grad_params
    new_second = beta_two * second_moment + (1.0 - beta_two) * grad_params * grad_params
    first_hat = new_first / (1.0 - beta_one ** STEP)
    second_hat = new_second / (1.0 - beta_two ** STEP)
    marks = pack_layout(zero_parts[0], zero_parts[1], zero_parts[2], zero_parts[3], jnp.ones((D,), jnp.float32), jnp.ones((D,), jnp.float32))
    gain_part = marks > 0.5
    step_rate = jnp.where(gain_part, gain_rate, matrix_rate)
    decay_rate = jnp.where(gain_part, 0.0, matrix_decay)
    direction = first_hat / (jnp.sqrt(second_hat) + adam_eps)
    new_params = params - step_rate * (direction + decay_rate * params)
    return (outputs.reshape(SEQS, LENGTH, D), grad_inputs.reshape(SEQS, LENGTH, D), grad_params, new_params, new_first, new_second)
```

```python
import math

import jax
import jax.numpy as jnp
from jax import lax
from jax.experimental import pallas as pl
from jax.experimental.pallas import tpu as pltpu
from jax.sharding import PartitionSpec as P

D = 768
FF = 1152
HEAD = 64
HALF_WIN = 64
STEP = 3


norm_eps = 1e-05
beta_one = 0.9
beta_two = 0.98
adam_eps = 1e-06
rope_base = 10000.0
matrix_rate = 0.01
matrix_decay = 0.1
gain_rate = 0.1
masked_score = -1e30


def norm_forward(values):
    centred = values - jnp.mean(values, axis=-1, keepdims=True)
    inverse = lax.rsqrt(jnp.mean(centred * centred, axis=-1, keepdims=True) + norm_eps)
    return (centred * inverse, inverse)


def norm_backward(grad_norm, gain_vec, normed, inverse):
    scaled = grad_norm * gain_vec
    return inverse * (
        scaled
        - jnp.mean(scaled, axis=-1, keepdims=True)
        - normed * jnp.mean(scaled * normed, axis=-1, keepdims=True)
    )


def rotary_tables(length):
    position = lax.iota(jnp.float32, length)
    exponent = lax.iota(jnp.float32, HEAD // 2) * (2.0 / HEAD)
    inv_freq = jnp.exp(-math.log(rope_base) * exponent)
    phases = position[:, None] * inv_freq[None, :]
    cosine = jnp.concatenate([jnp.cos(phases), jnp.cos(phases)], axis=-1)[:, None, :]
    sine_table = jnp.concatenate([jnp.sin(phases), jnp.sin(phases)], axis=-1)[:, None, :]
    return (cosine, sine_table)


def rotate_half(values):
    middle = values.shape[-1] // 2
    return jnp.concatenate([-values[..., middle:], values[..., :middle]], axis=-1)


def rotate_back(values):
    middle = values.shape[-1] // 2
    return jnp.concatenate([values[..., middle:], -values[..., :middle]], axis=-1)


def gelu_parts(values):
    cdf_part = 0.5 * (1.0 + jax.scipy.special.erf(values * (1.0 / math.sqrt(2.0))))
    pdf_part = jnp.exp(-0.5 * values * values) * (1.0 / math.sqrt(2.0 * math.pi))
    return (values * cdf_part, cdf_part + values * pdf_part)


def window_keys(values, block_rows):
    seq_count, length = (values.shape[0], values.shape[1])
    padded = jnp.pad(values, ((0, 0), (block_rows // 2, block_rows // 2), (0, 0), (0, 0)))
    blocks = padded.reshape(
        seq_count, length // block_rows + 1, block_rows, values.shape[2], values.shape[3]
    )
    return jnp.concatenate([blocks[:, :-1], blocks[:, 1:]], axis=2)


def fold_keys(windows, block_rows):
    seq_count, block_count = (windows.shape[0], windows.shape[1])
    zeros_block = jnp.zeros_like(windows[:, :1, :block_rows])
    low_part = jnp.concatenate([windows[:, :, :block_rows], zeros_block], axis=1)
    high_part = jnp.concatenate([zeros_block, windows[:, :, block_rows:]], axis=1)
    merged = (low_part + high_part).reshape(
        seq_count, (block_count + 1) * block_rows, windows.shape[3], windows.shape[4]
    )
    return merged[:, block_rows // 2 : block_rows // 2 + block_count * block_rows]


def band_mask(length, block_rows):
    block_count = length // block_rows
    dims = (block_count, block_rows, 2 * block_rows)
    query_pos = lax.broadcasted_iota(jnp.int32, dims, 1)
    key_pos = lax.broadcasted_iota(jnp.int32, dims, 2)
    block_pos = lax.broadcasted_iota(jnp.int32, dims, 0)
    relative = key_pos - query_pos
    absolute = block_pos * block_rows - block_rows // 2 + key_pos
    return (relative >= 0) & (relative <= block_rows) & (absolute >= 0) & (absolute < length)


MESH = pl.DeviceIdType.MESH
VM = pl.BlockSpec(memory_space=pltpu.VMEM)
PIECES = 4


def remote(src, dst, send_sem, recv_sem, axis, index):
    return pltpu.make_async_remote_copy(
        src_ref=src,
        dst_ref=dst,
        send_sem=send_sem,
        recv_sem=recv_sem,
        device_id={axis: index},
        device_id_type=MESH,
    )


def greet(targets):
    barrier = pltpu.get_barrier_semaphore()
    for axis, index in targets:
        pl.semaphore_signal(barrier, inc=1, device_id={axis: index}, device_id_type=MESH)
    pl.semaphore_wait(barrier, len(targets))


def zero_places():
    me = lax.axis_index("zero")
    chip, core = me // 2, me % 2
    mate = chip * 2 + 1 - core
    across = (1 - chip) * 2 + core
    diagonal = (1 - chip) * 2 + 1 - core
    return me, mate, across, diagonal


def zero_gather_kernel(x_ref, out_ref, own_sem, send_sem, recv_sem, far_send, far_recv, fwd_send, fwd_recv):
    me, mate, across, diagonal = zero_places()
    rows = x_ref.shape[0]
    part = rows // PIECES
    greet([("zero", mate), ("zero", across)])
    far, fwd = [], []
    for k in range(PIECES):
        copy = remote(
            x_ref.at[pl.ds(k * part, part)],
            out_ref.at[me, pl.ds(k * part, part)],
            far_send.at[k],
            far_recv.at[k],
            "zero",
            across,
        )
        copy.start()
        far.append(copy)
    near = remote(x_ref, out_ref.at[me], send_sem, recv_sem, "zero", mate)
    near.start()
    own = pltpu.make_async_copy(x_ref, out_ref.at[me], own_sem)
    own.start()
    for k in range(PIECES):
        far[k].wait_recv()
        piece = out_ref.at[across, pl.ds(k * part, part)]
        copy = remote(piece, piece, fwd_send.at[k], fwd_recv.at[k], "zero", mate)
        copy.start()
        fwd.append(copy)
    own.wait()
    near.wait()
    for k in range(PIECES):
        far[k].wait_send()
        fwd[k].wait()


def zero_gather(x, collective_id):
    zero_count = lax.axis_size("zero")
    rows, width = x.shape
    out = pl.pallas_call(
        zero_gather_kernel,
        out_shape=jax.ShapeDtypeStruct((zero_count, rows, width), x.dtype),
        in_specs=[VM],
        out_specs=VM,
        scratch_shapes=[pltpu.SemaphoreType.DMA] * 3 + [pltpu.SemaphoreType.DMA((PIECES,))] * 4,
        compiler_params=pltpu.CompilerParams(collective_id=collective_id, has_side_effects=True),
    )(x)
    return out.reshape(zero_count * rows, width)


def zero_scatter_kernel(
    terms_ref, out_ref, mine, mixed, total, far, mate_send, mate_recv, mix_send, mix_recv, far_send, far_recv
):
    me, mate, across, diagonal = zero_places()
    rows = terms_ref.shape[1]
    part = rows // PIECES
    greet([("zero", mate), ("zero", across)])
    mixes, fars = [], []
    for k in range(PIECES):
        copy = remote(
            terms_ref.at[diagonal, pl.ds(k * part, part)],
            mixed.at[pl.ds(k * part, part)],
            mix_send.at[k],
            mix_recv.at[k],
            "zero",
            mate,
        )
        copy.start()
        mixes.append(copy)
    near = remote(terms_ref.at[mate], mine, mate_send, mate_recv, "zero", mate)
    near.start()
    for k in range(PIECES):
        mixes[k].wait_recv()
        piece = pl.ds(k * part, part)
        total[piece] = (
            terms_ref[across, piece].astype(jnp.float32) + mixed[piece].astype(jnp.float32)
        ).astype(jnp.bfloat16)
        copy = remote(
            total.at[piece], far.at[piece], far_send.at[k], far_recv.at[k], "zero", across
        )
        copy.start()
        fars.append(copy)
    near.wait()
    for k in range(PIECES):
        piece = pl.ds(k * part, part)
        fars[k].wait_recv()
        out_ref[piece] = (
            terms_ref[me, piece].astype(jnp.float32)
            + mine[piece].astype(jnp.float32)
            + far[piece].astype(jnp.float32)
        )
    for k in range(PIECES):
        mixes[k].wait_send()
        fars[k].wait_send()


def zero_scatter(terms, collective_id):
    zero_count = lax.axis_size("zero")
    rows, width = terms.shape[0] // zero_count, terms.shape[1]
    buf = pltpu.VMEM((rows, width), jnp.bfloat16)
    return pl.pallas_call(
        zero_scatter_kernel,
        out_shape=jax.ShapeDtypeStruct((rows, width), jnp.float32),
        in_specs=[VM],
        out_specs=VM,
        scratch_shapes=[buf] * 4
        + [pltpu.SemaphoreType.DMA] * 2
        + [pltpu.SemaphoreType.DMA((PIECES,))] * 4,
        compiler_params=pltpu.CompilerParams(collective_id=collective_id, has_side_effects=True),
    )(terms.reshape(zero_count, rows, width))


def shift_kernel(step, x_ref, out_ref):
    x = x_ref[...]
    rows, width = x.shape
    shift = lax.axis_index("dp") * step
    rolled = pltpu.roll(x, shift, axis=1)
    above = pltpu.roll(rolled, 1, axis=0)
    lane = lax.broadcasted_iota(jnp.int32, x.shape, 1)
    out_ref[pl.ds(0, rows)] = jnp.where(lane >= shift, rolled, above).astype(out_ref.dtype)
    if out_ref.shape[0] > rows:
        out_ref[pl.ds(rows, out_ref.shape[0] - rows)] = jnp.zeros(
            (out_ref.shape[0] - rows, width), out_ref.dtype
        )


def shift_piece(x, step, out_rows):
    return pl.pallas_call(
        lambda *refs: shift_kernel(step, *refs),
        out_shape=jax.ShapeDtypeStruct((out_rows, x.shape[1]), jnp.bfloat16),
        in_specs=[VM],
        out_specs=VM,
        name="shift_piece",
    )(x)


def dp_gather_kernel(
    tail, x_ref, out_ref, gains_ref, own_sem, own_gain, z_send, z_recv, y_send, y_recv, g_send, g_recv
):
    me = lax.axis_index("dp")
    count = out_ref.shape[0]
    columns = count // 2
    z_me, y_me = me // 2, me % 2
    peer = z_me * 2 + 1 - y_me
    spread = [lax.rem(z_me + k, columns) * 2 + y_me for k in range(1, columns)]
    origin = [lax.rem(z_me + columns - k, columns) * 2 + y_me for k in range(1, columns)]
    zero_me = lax.axis_index("zero")
    zero_count = gains_ref.shape[0]
    others = [lax.rem(zero_me + k, zero_count) for k in range(1, zero_count)]
    greet([("dp", peer)] + [("dp", i) for i in spread] + [("zero", i) for i in others])
    own = pltpu.make_async_copy(x_ref, out_ref.at[me], own_sem)
    own.start()
    first = remote(x_ref, out_ref.at[me], y_send.at[0], y_recv.at[0], "dp", peer)
    first.start()
    zs, ys = [], []
    for k in range(columns - 1):
        copy = remote(x_ref, out_ref.at[me], z_send.at[k], z_recv.at[k], "dp", spread[k])
        copy.start()
        zs.append(copy)
    for k in (0, columns - 2) + tuple(range(1, columns - 2)):
        zs[k].wait_recv()
        piece = out_ref.at[origin[k]]
        copy = remote(piece, piece, y_send.at[k + 1], y_recv.at[k + 1], "dp", peer)
        copy.start()
        ys.append(copy)
    own.wait()
    first.wait()
    for copy in ys:
        copy.wait()
    last = out_ref.at[count - 1, pl.ds(tail, 16)]
    own = pltpu.make_async_copy(last, gains_ref.at[zero_me], own_gain)
    own.start()
    gs = []
    for k in range(zero_count - 1):
        copy = remote(last, gains_ref.at[zero_me], g_send.at[k], g_recv.at[k], "zero", others[k])
        copy.start()
        gs.append(copy)
    own.wait()
    for copy in gs:
        copy.wait()
    for copy in zs:
        copy.wait_send()


def dp_gather(x, tail, collective_id):
    count, zero_count = lax.axis_size("dp"), lax.axis_size("zero")
    columns = count // 2
    rows, width = x.shape
    dma = pltpu.SemaphoreType.DMA
    return pl.pallas_call(
        lambda *refs: dp_gather_kernel(tail, *refs),
        out_shape=(
            jax.ShapeDtypeStruct((count, rows, width), x.dtype),
            jax.ShapeDtypeStruct((zero_count, 16, width), x.dtype),
        ),
        in_specs=[VM],
        out_specs=(VM, VM),
        scratch_shapes=[
            dma,
            dma,
            dma((columns - 1,)),
            dma((columns - 1,)),
            dma((columns,)),
            dma((columns,)),
            dma((zero_count - 1,)),
            dma((zero_count - 1,)),
        ],
        compiler_params=pltpu.CompilerParams(collective_id=collective_id, has_side_effects=True),
        name="dp_gather",
    )(x)


def dp_scatter_kernel(step, x_ref, out_ref, pair, total, far, y_send, y_recv, z_send, z_recv):
    me = lax.axis_index("dp")
    count, rows, width = x_ref.shape
    columns = count // 2
    z_me, y_me = me // 2, me % 2
    peer = z_me * 2 + 1 - y_me
    order = [lax.rem(z_me + k, columns) for k in (*range(1, columns), 0)]
    greet([("dp", peer)] + [("dp", z * 2 + y_me) for z in order[:-1]])
    ys, zs = [], []
    for k in range(columns):
        copy = remote(
            x_ref.at[order[k] * 2 + 1 - y_me], pair.at[k], y_send.at[k], y_recv.at[k], "dp", peer
        )
        copy.start()
        ys.append(copy)
    for k in range(columns - 1):
        ys[k].wait_recv()
        total[k] = (
            x_ref[order[k] * 2 + y_me].astype(jnp.float32) + pair[k].astype(jnp.float32)
        ).astype(jnp.bfloat16)
        copy = remote(
            total.at[k], far.at[k], z_send.at[k], z_recv.at[k], "dp", order[k] * 2 + y_me
        )
        copy.start()
        zs.append(copy)
    ys[columns - 1].wait_recv()
    acc = x_ref[me].astype(jnp.float32) + pair[columns - 1].astype(jnp.float32)
    for k in range(columns - 1):
        zs[k].wait_recv()
        acc = acc + far[k].astype(jnp.float32)
    if step:
        shift = me * step
        rolled = pltpu.roll(acc, lax.rem(width - shift, width), axis=1)
        below = pltpu.roll(rolled, rows - 1, axis=0)
        lane = lax.broadcasted_iota(jnp.int32, acc.shape, 1)
        acc = jnp.where(lane + shift < width, rolled, below)
    out_ref[...] = acc
    for copy in ys:
        copy.wait_send()
    for copy in zs:
        copy.wait_send()


def dp_scatter(x, step, collective_id):
    count, rows, width = x.shape
    columns = count // 2
    dma = pltpu.SemaphoreType.DMA
    return pl.pallas_call(
        lambda *refs: dp_scatter_kernel(step, *refs),
        out_shape=jax.ShapeDtypeStruct((rows, width), jnp.float32),
        in_specs=[VM],
        out_specs=VM,
        scratch_shapes=[
            pltpu.VMEM((columns, rows, width), x.dtype),
            pltpu.VMEM((columns - 1, rows, width), x.dtype),
            pltpu.VMEM((columns - 1, rows, width), x.dtype),
            dma((columns,)),
            dma((columns,)),
            dma((columns - 1,)),
            dma((columns - 1,)),
        ],
        compiler_params=pltpu.CompilerParams(collective_id=collective_id, has_side_effects=True),
        name="dp_scatter",
    )(x)


def per_device(tokens, cotangent, params, first_moment, second_moment):
    zero_count = lax.axis_size("zero")
    dp_count = lax.axis_size("dp")
    shard_size = params.shape[2]
    quarter = D // zero_count
    ff_part = FF // zero_count
    ffn_piece = 3 * D * FF // zero_count // dp_count
    attn_piece = shard_size - ffn_piece
    attn_rows, attn_step = attn_piece // D, attn_piece % D
    aligned = ffn_piece % D == 0 and attn_rows % 16 == 0 and dp_count == 8
    lift_end = 2 * ff_part * D
    first_end = 3 * quarter * D
    second_end = first_end + D * quarter
    if aligned:
        own = params.reshape(shard_size)
        ffn_own = own[:ffn_piece].reshape(ffn_piece // D, D).astype(jnp.bfloat16)
        pad_rows = attn_rows + 8
        attn_own = jnp.pad(own[ffn_piece:], (0, pad_rows * D - attn_piece)).reshape(pad_rows, D)
        attn_own = shift_piece(attn_own, attn_step, attn_rows + 16)
        attn_all, gain_rows = dp_gather(attn_own, attn_rows, 1)
        ffn_all = lax.all_gather(ffn_own, "dp", axis=0, tiled=True)
        edge = jnp.concatenate([jnp.zeros((1, D), jnp.bfloat16), attn_all[:-1, attn_rows]])
        body = attn_all[:, :attn_rows]
        lead = lax.broadcasted_iota(jnp.int32, body.shape, 1) == 0
        body = body + jnp.where(lead, edge[:, None, :], jnp.zeros((), jnp.bfloat16))
        body = body.reshape(dp_count * attn_rows, D)
        w_qkv = body[: 3 * quarter]
        w_attn = body[3 * quarter :].reshape(D, quarter)
        gains = gain_rows[:, 0, : 2 * quarter].reshape(zero_count, 2, quarter)
        gains = jnp.transpose(gains, (1, 0, 2)).reshape(2, D)
        w_input = ffn_all[: 2 * ff_part]
        w_output = ffn_all[2 * ff_part :].reshape(D, ff_part)
    else:
        own_bf = params.astype(jnp.bfloat16)
        slice_all = lax.all_gather(own_bf, "dp", axis=1, tiled=True).reshape(dp_count, shard_size)
        ffn_flat = slice_all[:, :ffn_piece].reshape(-1)
        attn_flat = slice_all[:, ffn_piece:].reshape(-1)
        w_qkv = attn_flat[:first_end].reshape(3 * quarter, D)
        w_attn = attn_flat[first_end:second_end].reshape(D, quarter)
        gains = lax.all_gather(
            attn_flat[second_end:].reshape(2, quarter), "zero", axis=1, tiled=True
        )
        w_input = ffn_flat[:lift_end].reshape(2 * ff_part, D)
        w_output = ffn_flat[lift_end:].reshape(D, ff_part)
    gain_one32 = gains[0].astype(jnp.float32)
    gain_two32 = gains[1].astype(jnp.float32)
    seq_count, own_len = (tokens.shape[0], tokens.shape[1])
    own_rows = seq_count * own_len
    length = own_len * zero_count
    row_count = seq_count * length
    local_heads = quarter // HEAD
    block_rows = 2 * HALF_WIN
    block_count = length // block_rows
    cosine, sine_table = rotary_tables(length)
    allowed = band_mask(length, block_rows)[None, :, None]
    inputs = tokens.astype(jnp.float32).reshape(own_rows, D)
    normed_one, inverse_one = norm_forward(inputs)
    normal_one = (normed_one * gain_one32).astype(jnp.bfloat16).reshape(seq_count, own_len, D)
    full_one = zero_gather(normal_one.reshape(own_rows, D), 2)
    projected = jnp.dot(full_one, w_qkv.T, preferred_element_type=jnp.float32)
    projected = projected.reshape(seq_count, length, 3, local_heads, HEAD)
    queries = (projected[:, :, 0] * cosine + rotate_half(projected[:, :, 0]) * sine_table).astype(
        jnp.bfloat16
    )
    key_rows = (projected[:, :, 1] * cosine + rotate_half(projected[:, :, 1]) * sine_table).astype(
        jnp.bfloat16
    )
    value_rows = projected[:, :, 2].astype(jnp.bfloat16)
    query_blocks = queries.reshape(seq_count, block_count, block_rows, local_heads, HEAD)
    key_windows = window_keys(key_rows, block_rows)
    value_windows = window_keys(value_rows, block_rows)
    scores = (
        jnp.einsum(
            "sbqhe,sbkhe->sbhqk", query_blocks, key_windows, preferred_element_type=jnp.float32
        )
        * 0.125
    )
    scores = jnp.where(allowed, scores, masked_score)
    row_max = jnp.max(scores, axis=-1, keepdims=True)
    log_total = row_max + jnp.log(jnp.sum(jnp.exp(scores - row_max), axis=-1, keepdims=True))
    attn_probs = jnp.exp(scores - log_total).astype(jnp.bfloat16)
    context = jnp.einsum(
        "sbhqk,sbkhe->sbqhe", attn_probs, value_windows, preferred_element_type=jnp.float32
    ).astype(jnp.bfloat16)
    context_rows = context.reshape(row_count, quarter)
    attn_terms = jnp.dot(context_rows, w_attn.T, preferred_element_type=jnp.float32)
    attn_sum = zero_scatter(attn_terms.astype(jnp.bfloat16), 6)
    hidden = inputs + attn_sum.reshape(own_rows, D)
    normed_two, inverse_two = norm_forward(hidden)
    normal_two = (normed_two * gain_two32).astype(jnp.bfloat16).reshape(seq_count, own_len, D)
    full_two = zero_gather(normal_two.reshape(own_rows, D), 3)
    lifted = jnp.dot(full_two, w_input.T, preferred_element_type=jnp.float32)
    gate_act, gate_slope = gelu_parts(lifted[:, :ff_part])
    up_half = lifted[:, ff_part:]
    mixed = (gate_act * up_half).astype(jnp.bfloat16)
    ffn_terms = jnp.dot(mixed, w_output.T, preferred_element_type=jnp.float32)
    ffn_sum = zero_scatter(ffn_terms.astype(jnp.bfloat16), 7)
    output = hidden + ffn_sum.reshape(own_rows, D)
    grad_scale = float(dp_count * row_count) ** (-0.5)
    cot_full = lax.all_gather(cotangent, "zero", axis=1, tiled=True).reshape(row_count, D)
    grad_output_w = jnp.dot(cot_full.T, mixed, preferred_element_type=jnp.float32)
    grad_mixed = jnp.dot(cot_full, w_output, preferred_element_type=jnp.float32)
    grad_lifted = jnp.concatenate(
        [grad_mixed * up_half * gate_slope, grad_mixed * gate_act], axis=-1
    ).astype(jnp.bfloat16)
    grad_input_w = jnp.dot(grad_lifted.T, full_two, preferred_element_type=jnp.float32)
    if aligned:
        ffn_grads = jnp.concatenate([grad_input_w, grad_output_w.reshape(ff_part, D)]) * grad_scale
        ffn_shard = lax.psum_scatter(
            ffn_grads.astype(jnp.bfloat16), "dp", scatter_dimension=0, tiled=True
        ).astype(jnp.float32)
    else:
        ffn_vec = jnp.concatenate([grad_input_w.ravel(), grad_output_w.ravel()]) * grad_scale
        ffn_vec = ffn_vec.reshape(dp_count, ffn_piece)
    norm_two_terms = jnp.dot(grad_lifted, w_input, preferred_element_type=jnp.float32)
    grad_norm_two = zero_scatter(norm_two_terms.astype(jnp.bfloat16), 8)
    gain_two_term = jnp.sum(grad_norm_two * normed_two, axis=0)
    grad_hidden = cotangent.reshape(own_rows, D).astype(jnp.float32) + norm_backward(
        grad_norm_two, gain_two32, normed_two, inverse_two
    )
    grad_hidden_b = grad_hidden.astype(jnp.bfloat16).reshape(seq_count, own_len, D)
    hidden_full = zero_gather(grad_hidden_b.reshape(own_rows, D), 5)
    grad_attn_w = jnp.dot(hidden_full.T, context_rows, preferred_element_type=jnp.float32)
    grad_context = jnp.dot(hidden_full, w_attn, preferred_element_type=jnp.float32).astype(
        jnp.bfloat16
    )
    grad_context = grad_context.reshape(seq_count, block_count, block_rows, local_heads, HEAD)
    again = (
        jnp.einsum(
            "sbqhe,sbkhe->sbhqk", query_blocks, key_windows, preferred_element_type=jnp.float32
        )
        * 0.125
    )
    probs_full = jnp.exp(jnp.where(allowed, again, masked_score) - log_total)
    grad_probs = jnp.einsum(
        "sbqhe,sbkhe->sbhqk", grad_context, value_windows, preferred_element_type=jnp.float32
    )
    row_term = jnp.sum(grad_context.astype(jnp.float32) * context.astype(jnp.float32), axis=-1)
    row_term = jnp.transpose(row_term, (0, 1, 3, 2))[..., None]
    grad_scores = (probs_full * (grad_probs - row_term) * 0.125).astype(jnp.bfloat16)
    probs_b = probs_full.astype(jnp.bfloat16)
    grad_query = jnp.einsum(
        "sbhqk,sbkhe->sbqhe", grad_scores, key_windows, preferred_element_type=jnp.float32
    ).reshape(seq_count, length, local_heads, HEAD)
    grad_key = fold_keys(
        jnp.einsum(
            "sbhqk,sbqhe->sbkhe", grad_scores, query_blocks, preferred_element_type=jnp.float32
        ),
        block_rows,
    )
    grad_value = fold_keys(
        jnp.einsum("sbhqk,sbqhe->sbkhe", probs_b, grad_context, preferred_element_type=jnp.float32),
        block_rows,
    )
    grad_query = grad_query * cosine + rotate_back(grad_query * sine_table)
    grad_key = grad_key * cosine + rotate_back(grad_key * sine_table)
    grad_packed = (
        jnp.stack([grad_query, grad_key, grad_value], axis=2)
        .astype(jnp.bfloat16)
        .reshape(row_count, 3 * quarter)
    )
    grad_qkv_w = jnp.dot(grad_packed.T, full_one, preferred_element_type=jnp.float32)
    norm_one_terms = jnp.dot(grad_packed, w_qkv, preferred_element_type=jnp.float32)
    grad_norm_one = zero_scatter(norm_one_terms.astype(jnp.bfloat16), 9)
    gain_one_term = jnp.sum(grad_norm_one * normed_one, axis=0)
    grad_inputs = grad_hidden + norm_backward(grad_norm_one, gain_one32, normed_one, inverse_one)
    gain_grads = lax.psum_scatter(
        jnp.stack([gain_one_term, gain_two_term]), "zero", scatter_dimension=1, tiled=True
    )
    if aligned:
        gain_row = jnp.pad(gain_grads.reshape(1, 2 * quarter), ((0, 0), (0, D - 2 * quarter)))
        grad_rows = jnp.concatenate([grad_qkv_w, grad_attn_w.reshape(quarter, D), gain_row])
        grad_rows = (grad_rows * grad_scale).astype(jnp.bfloat16)
        chunks = grad_rows[:-1].reshape(dp_count, attn_rows, D)
        chunks = jnp.concatenate(
            [
                chunks,
                jnp.concatenate([chunks[1:, :1], grad_rows[-1:][None]]),
                jnp.zeros((dp_count, 15, D), jnp.bfloat16),
            ],
            axis=1,
        )
        attn_shard = dp_scatter(chunks, attn_step, 10).reshape(-1)[:attn_piece]
        grad_shard = jnp.concatenate([ffn_shard.reshape(-1), attn_shard])
    else:
        attn_vec = (
            jnp.concatenate([grad_qkv_w.ravel(), grad_attn_w.ravel(), gain_grads.ravel()])
            * grad_scale
        )
        attn_vec = attn_vec.reshape(dp_count, attn_piece)
        grad_shard = lax.psum_scatter(
            jnp.concatenate([ffn_vec, attn_vec], axis=1), "dp", scatter_dimension=0, tiled=True
        )
    grad_shard = grad_shard.reshape(params.shape)
    new_first = beta_one * first_moment + (1.0 - beta_one) * grad_shard
    new_second = beta_two * second_moment + (1.0 - beta_two) * grad_shard * grad_shard
    first_hat = new_first / (1.0 - beta_one**STEP)
    second_hat = new_second / (1.0 - beta_two**STEP)
    attn_total = attn_piece * dp_count
    place = lax.axis_index("dp") * attn_piece + lax.iota(jnp.int32, attn_piece)
    gain_tail = place >= attn_total - 2 * quarter
    gain_part = jnp.concatenate([jnp.zeros((ffn_piece,), jnp.bool_), gain_tail]).reshape(
        params.shape
    )
    step_rate = jnp.where(gain_part, gain_rate, matrix_rate)
    decay_rate = jnp.where(gain_part, 0.0, matrix_decay)
    direction = first_hat / (jnp.sqrt(second_hat) + adam_eps)
    new_params = params - step_rate * (direction + decay_rate * params)
    return (
        output.astype(jnp.bfloat16).reshape(tokens.shape),
        grad_inputs.reshape(tokens.shape),
        grad_shard,
        new_params,
        new_first,
        new_second,
    )


def solution(mesh):
    in_specs = (
        P("dp", "zero", None),
        P("dp", "zero", None),
        P("zero", "dp", None),
        P("zero", "dp", None),
        P("zero", "dp", None),
    )
    out_specs = (
        P("dp", "zero", None),
        P("dp", "zero", None),
        P("zero", "dp", None),
        P("zero", "dp", None),
        P("zero", "dp", None),
        P("zero", "dp", None),
    )
    return jax.shard_map(
        per_device, mesh=mesh, in_specs=in_specs, out_specs=out_specs, check_vma=False
    )
```

```python
import math

import jax
import jax.numpy as jnp
from jax import lax
from jax.experimental import pallas as pl
from jax.experimental.pallas import tpu as pltpu
from jax.sharding import PartitionSpec as P

D = 768
FF = 1152
HEAD = 64
HALF_WIN = 64
STEP = 3


norm_eps = 1e-05
beta_one = 0.9
beta_two = 0.98
adam_eps = 1e-06
rope_base = 10000.0
matrix_rate = 0.01
matrix_decay = 0.1
gain_rate = 0.1
masked_score = -1e30


def norm_forward(values):
    centred = values - jnp.mean(values, axis=-1, keepdims=True)
    inverse = lax.rsqrt(jnp.mean(centred * centred, axis=-1, keepdims=True) + norm_eps)
    return (centred * inverse, inverse)


def norm_backward(grad_norm, gain_vec, normed, inverse):
    scaled = grad_norm * gain_vec
    return inverse * (
        scaled
        - jnp.mean(scaled, axis=-1, keepdims=True)
        - normed * jnp.mean(scaled * normed, axis=-1, keepdims=True)
    )


def rotary_tables(length):
    position = lax.iota(jnp.float32, length)
    exponent = lax.iota(jnp.float32, HEAD // 2) * (2.0 / HEAD)
    inv_freq = jnp.exp(-math.log(rope_base) * exponent)
    phases = position[:, None] * inv_freq[None, :]
    cosine = jnp.concatenate([jnp.cos(phases), jnp.cos(phases)], axis=-1)[:, None, :]
    sine_table = jnp.concatenate([jnp.sin(phases), jnp.sin(phases)], axis=-1)[:, None, :]
    return (cosine, sine_table)


def rotate_half(values):
    middle = values.shape[-1] // 2
    return jnp.concatenate([-values[..., middle:], values[..., :middle]], axis=-1)


def rotate_back(values):
    middle = values.shape[-1] // 2
    return jnp.concatenate([values[..., middle:], -values[..., :middle]], axis=-1)


def gelu_parts(values):
    cdf_part = 0.5 * (1.0 + jax.scipy.special.erf(values * (1.0 / math.sqrt(2.0))))
    pdf_part = jnp.exp(-0.5 * values * values) * (1.0 / math.sqrt(2.0 * math.pi))
    return (values * cdf_part, cdf_part + values * pdf_part)


def window_keys(values, block_rows):
    seq_count, length = (values.shape[0], values.shape[1])
    padded = jnp.pad(values, ((0, 0), (block_rows // 2, block_rows // 2), (0, 0), (0, 0)))
    blocks = padded.reshape(
        seq_count, length // block_rows + 1, block_rows, values.shape[2], values.shape[3]
    )
    return jnp.concatenate([blocks[:, :-1], blocks[:, 1:]], axis=2)


def fold_keys(windows, block_rows):
    seq_count, block_count = (windows.shape[0], windows.shape[1])
    zeros_block = jnp.zeros_like(windows[:, :1, :block_rows])
    low_part = jnp.concatenate([windows[:, :, :block_rows], zeros_block], axis=1)
    high_part = jnp.concatenate([zeros_block, windows[:, :, block_rows:]], axis=1)
    merged = (low_part + high_part).reshape(
        seq_count, (block_count + 1) * block_rows, windows.shape[3], windows.shape[4]
    )
    return merged[:, block_rows // 2 : block_rows // 2 + block_count * block_rows]


def band_mask(length, block_rows):
    block_count = length // block_rows
    dims = (block_count, block_rows, 2 * block_rows)
    query_pos = lax.broadcasted_iota(jnp.int32, dims, 1)
    key_pos = lax.broadcasted_iota(jnp.int32, dims, 2)
    block_pos = lax.broadcasted_iota(jnp.int32, dims, 0)
    relative = key_pos - query_pos
    absolute = block_pos * block_rows - block_rows // 2 + key_pos
    return (relative >= 0) & (relative <= block_rows) & (absolute >= 0) & (absolute < length)


MESH = pl.DeviceIdType.MESH
VM = pl.BlockSpec(memory_space=pltpu.VMEM)
PIECES = 4


def remote(src, dst, send_sem, recv_sem, axis, index):
    return pltpu.make_async_remote_copy(
        src_ref=src,
        dst_ref=dst,
        send_sem=send_sem,
        recv_sem=recv_sem,
        device_id={axis: index},
        device_id_type=MESH,
    )


def greet(targets):
    barrier = pltpu.get_barrier_semaphore()
    for axis, index in targets:
        pl.semaphore_signal(barrier, inc=1, device_id={axis: index}, device_id_type=MESH)
    pl.semaphore_wait(barrier, len(targets))


def zero_places():
    me = lax.axis_index("zero")
    chip, core = me // 2, me % 2
    mate = chip * 2 + 1 - core
    across = (1 - chip) * 2 + core
    diagonal = (1 - chip) * 2 + 1 - core
    return me, mate, across, diagonal


def zero_gather_kernel(x_ref, out_ref, own_sem, send_sem, recv_sem, far_send, far_recv, fwd_send, fwd_recv):
    me, mate, across, diagonal = zero_places()
    rows = x_ref.shape[0]
    part = rows // PIECES
    greet([("zero", mate), ("zero", across)])
    far, fwd = [], []
    for k in range(PIECES):
        copy = remote(
            x_ref.at[pl.ds(k * part, part)],
            out_ref.at[me, pl.ds(k * part, part)],
            far_send.at[k],
            far_recv.at[k],
            "zero",
            across,
        )
        copy.start()
        far.append(copy)
    near = remote(x_ref, out_ref.at[me], send_sem, recv_sem, "zero", mate)
    near.start()
    own = pltpu.make_async_copy(x_ref, out_ref.at[me], own_sem)
    own.start()
    for k in range(PIECES):
        far[k].wait_recv()
        piece = out_ref.at[across, pl.ds(k * part, part)]
        copy = remote(piece, piece, fwd_send.at[k], fwd_recv.at[k], "zero", mate)
        copy.start()
        fwd.append(copy)
    own.wait()
    near.wait()
    for k in range(PIECES):
        far[k].wait_send()
        fwd[k].wait()


def zero_gather(x, collective_id):
    zero_count = lax.axis_size("zero")
    rows, width = x.shape
    out = pl.pallas_call(
        zero_gather_kernel,
        out_shape=jax.ShapeDtypeStruct((zero_count, rows, width), x.dtype),
        in_specs=[VM],
        out_specs=VM,
        scratch_shapes=[pltpu.SemaphoreType.DMA] * 3 + [pltpu.SemaphoreType.DMA((PIECES,))] * 4,
        compiler_params=pltpu.CompilerParams(collective_id=collective_id, has_side_effects=True),
    )(x)
    return out.reshape(zero_count * rows, width)


def zero_scatter_kernel(
    terms_ref, out_ref, mine, mixed, total, far, mate_send, mate_recv, mix_send, mix_recv, far_send, far_recv, extra=False
):
    me, mate, across, diagonal = zero_places()
    rows = terms_ref.shape[1]
    part = rows // PIECES
    greet([("zero", mate), ("zero", across)] + [("zero", diagonal)] * extra)
    mixes, fars = [], []
    for k in range(PIECES):
        copy = remote(
            terms_ref.at[diagonal, pl.ds(k * part, part)],
            mixed.at[pl.ds(k * part, part)],
            mix_send.at[k],
            mix_recv.at[k],
            "zero",
            mate,
        )
        copy.start()
        mixes.append(copy)
    near = remote(terms_ref.at[mate], mine, mate_send, mate_recv, "zero", mate)
    near.start()
    for k in range(PIECES):
        mixes[k].wait_recv()
        piece = pl.ds(k * part, part)
        total[piece] = (
            terms_ref[across, piece].astype(jnp.float32) + mixed[piece].astype(jnp.float32)
        ).astype(jnp.bfloat16)
        copy = remote(
            total.at[piece], far.at[piece], far_send.at[k], far_recv.at[k], "zero", across
        )
        copy.start()
        fars.append(copy)
    near.wait()
    for k in range(PIECES):
        piece = pl.ds(k * part, part)
        fars[k].wait_recv()
        out_ref[piece] = (
            terms_ref[me, piece].astype(jnp.float32)
            + mine[piece].astype(jnp.float32)
            + far[piece].astype(jnp.float32)
        )
    for k in range(PIECES):
        mixes[k].wait_send()
        fars[k].wait_send()


def zero_scatter(terms, collective_id):
    zero_count = lax.axis_size("zero")
    rows, width = terms.shape[0] // zero_count, terms.shape[1]
    buf = pltpu.VMEM((rows, width), jnp.bfloat16)
    return pl.pallas_call(
        zero_scatter_kernel,
        out_shape=jax.ShapeDtypeStruct((rows, width), jnp.float32),
        in_specs=[VM],
        out_specs=VM,
        scratch_shapes=[buf] * 4
        + [pltpu.SemaphoreType.DMA] * 2
        + [pltpu.SemaphoreType.DMA((PIECES,))] * 4,
        compiler_params=pltpu.CompilerParams(collective_id=collective_id, has_side_effects=True),
    )(terms.reshape(zero_count, rows, width))


def zero_scatter_gain_kernel(
    terms_ref,
    normed_ref,
    other_ref,
    out_ref,
    gain_ref,
    mine,
    mixed,
    total,
    far,
    gain_own,
    gain_in,
    mate_send,
    mate_recv,
    gain_send,
    gain_recv,
    *sems,
):
    me, mate, across, diagonal = zero_places()
    zero_scatter_kernel(
        terms_ref, out_ref, mine, mixed, total, far, mate_send, mate_recv, *sems, extra=True
    )
    gain_own[...] = jnp.zeros_like(gain_own)
    gain_own[pl.ds(0, 1)] = jnp.sum(out_ref[...] * normed_ref[...], axis=0, keepdims=True)
    gain_own[pl.ds(1, 1)] = other_ref[...]
    copies = []
    for k, index in enumerate((mate, across, diagonal)):
        copy = remote(gain_own, gain_in.at[k], gain_send.at[k], gain_recv.at[k], "zero", index)
        copy.start()
        copies.append(copy)
    total_gain = gain_own[...]
    for k, copy in enumerate(copies):
        copy.wait()
        total_gain = total_gain + gain_in[k]
    gain_ref[...] = total_gain


def zero_scatter_gain(terms, normed, other, collective_id):
    zero_count = lax.axis_size("zero")
    rows, width = terms.shape[0] // zero_count, terms.shape[1]
    buf = pltpu.VMEM((rows, width), jnp.bfloat16)
    dma = pltpu.SemaphoreType.DMA
    return pl.pallas_call(
        zero_scatter_gain_kernel,
        out_shape=(
            jax.ShapeDtypeStruct((rows, width), jnp.float32),
            jax.ShapeDtypeStruct((8, width), jnp.float32),
        ),
        in_specs=[VM] * 3,
        out_specs=(VM, VM),
        scratch_shapes=[buf] * 4
        + [pltpu.VMEM((8, width), jnp.float32), pltpu.VMEM((3, 8, width), jnp.float32)]
        + [dma] * 2
        + [dma((3,))] * 2
        + [dma((PIECES,))] * 4,
        compiler_params=pltpu.CompilerParams(collective_id=collective_id, has_side_effects=True),
    )(terms.reshape(zero_count, rows, width), normed, other)


def shift_kernel(step, x_ref, out_ref):
    x = x_ref[...]
    rows, width = x.shape
    shift = lax.axis_index("dp") * step
    rolled = pltpu.roll(x, shift, axis=1)
    above = pltpu.roll(rolled, 1, axis=0)
    lane = lax.broadcasted_iota(jnp.int32, x.shape, 1)
    out_ref[pl.ds(0, rows)] = jnp.where(lane >= shift, rolled, above).astype(out_ref.dtype)
    if out_ref.shape[0] > rows:
        out_ref[pl.ds(rows, out_ref.shape[0] - rows)] = jnp.zeros(
            (out_ref.shape[0] - rows, width), out_ref.dtype
        )


def shift_piece(x, step, out_rows):
    return pl.pallas_call(
        lambda *refs: shift_kernel(step, *refs),
        out_shape=jax.ShapeDtypeStruct((out_rows, x.shape[1]), jnp.bfloat16),
        in_specs=[VM],
        out_specs=VM,
        name="shift_piece",
    )(x)


def dp_gather_kernel(
    tail,
    x_ref,
    cot_ref,
    out_ref,
    gains_ref,
    cots_ref,
    own_sem,
    own_gain,
    own_cot,
    z_send,
    z_recv,
    y_send,
    y_recv,
    g_send,
    g_recv,
    c_send,
    c_recv,
):
    me = lax.axis_index("dp")
    count = out_ref.shape[0]
    columns = count // 2
    z_me, y_me = me // 2, me % 2
    peer = z_me * 2 + 1 - y_me
    spread = [lax.rem(z_me + k, columns) * 2 + y_me for k in range(1, columns)]
    origin = [lax.rem(z_me + columns - k, columns) * 2 + y_me for k in range(1, columns)]
    zero_me = lax.axis_index("zero")
    zero_count = gains_ref.shape[0]
    others = [lax.rem(zero_me + k, zero_count) for k in range(1, zero_count)]
    greet([("dp", peer)] + [("dp", i) for i in spread] + [("zero", i) for i in others])
    own = pltpu.make_async_copy(x_ref, out_ref.at[me], own_sem)
    own.start()
    first = remote(x_ref, out_ref.at[me], y_send.at[0], y_recv.at[0], "dp", peer)
    first.start()
    zs, ys = [], []
    for k in range(columns - 1):
        copy = remote(x_ref, out_ref.at[me], z_send.at[k], z_recv.at[k], "dp", spread[k])
        copy.start()
        zs.append(copy)
    own_c = pltpu.make_async_copy(cot_ref, cots_ref.at[zero_me], own_cot)
    own_c.start()
    cs = []
    for k in range(zero_count - 1):
        copy = remote(cot_ref, cots_ref.at[zero_me], c_send.at[k], c_recv.at[k], "zero", others[k])
        copy.start()
        cs.append(copy)
    for k in (0, columns - 2) + tuple(range(1, columns - 2)):
        zs[k].wait_recv()
        piece = out_ref.at[origin[k]]
        copy = remote(piece, piece, y_send.at[k + 1], y_recv.at[k + 1], "dp", peer)
        copy.start()
        ys.append(copy)
    own.wait()
    first.wait()
    for copy in ys:
        copy.wait()
    last = out_ref.at[count - 1, pl.ds(tail, 16)]
    own = pltpu.make_async_copy(last, gains_ref.at[zero_me], own_gain)
    own.start()
    gs = []
    for k in range(zero_count - 1):
        copy = remote(last, gains_ref.at[zero_me], g_send.at[k], g_recv.at[k], "zero", others[k])
        copy.start()
        gs.append(copy)
    own.wait()
    for copy in gs:
        copy.wait()
    own_c.wait()
    for copy in cs:
        copy.wait()
    for copy in zs:
        copy.wait_send()


def dp_gather(x, cot, tail, collective_id):
    count, zero_count = lax.axis_size("dp"), lax.axis_size("zero")
    columns = count // 2
    rows, width = x.shape
    dma = pltpu.SemaphoreType.DMA
    return pl.pallas_call(
        lambda *refs: dp_gather_kernel(tail, *refs),
        out_shape=(
            jax.ShapeDtypeStruct((count, rows, width), x.dtype),
            jax.ShapeDtypeStruct((zero_count, 16, width), x.dtype),
            jax.ShapeDtypeStruct((zero_count, *cot.shape), cot.dtype),
        ),
        in_specs=[VM, VM],
        out_specs=(VM, VM, VM),
        scratch_shapes=[
            dma,
            dma,
            dma,
            dma((columns - 1,)),
            dma((columns - 1,)),
            dma((columns,)),
            dma((columns,)),
            *[dma((zero_count - 1,))] * 4,
        ],
        compiler_params=pltpu.CompilerParams(collective_id=collective_id, has_side_effects=True),
        name="dp_gather",
    )(x, cot)


def dp_scatter_kernel(step, x_ref, out_ref, pair, total, far, y_send, y_recv, z_send, z_recv):
    me = lax.axis_index("dp")
    count, rows, width = x_ref.shape
    columns = count // 2
    z_me, y_me = me // 2, me % 2
    peer = z_me * 2 + 1 - y_me
    order = [lax.rem(z_me + k, columns) for k in (*range(1, columns), 0)]
    greet([("dp", peer)] + [("dp", z * 2 + y_me) for z in order[:-1]])
    ys, zs = [], []
    for k in range(columns):
        copy = remote(
            x_ref.at[order[k] * 2 + 1 - y_me], pair.at[k], y_send.at[k], y_recv.at[k], "dp", peer
        )
        copy.start()
        ys.append(copy)
    for k in range(columns - 1):
        ys[k].wait_recv()
        total[k] = (
            x_ref[order[k] * 2 + y_me].astype(jnp.float32) + pair[k].astype(jnp.float32)
        ).astype(jnp.bfloat16)
        copy = remote(
            total.at[k], far.at[k], z_send.at[k], z_recv.at[k], "dp", order[k] * 2 + y_me
        )
        copy.start()
        zs.append(copy)
    ys[columns - 1].wait_recv()
    acc = x_ref[me].astype(jnp.float32) + pair[columns - 1].astype(jnp.float32)
    for k in range(columns - 1):
        zs[k].wait_recv()
        acc = acc + far[k].astype(jnp.float32)
    if step:
        shift = me * step
        rolled = pltpu.roll(acc, lax.rem(width - shift, width), axis=1)
        below = pltpu.roll(rolled, rows - 1, axis=0)
        lane = lax.broadcasted_iota(jnp.int32, acc.shape, 1)
        acc = jnp.where(lane + shift < width, rolled, below)
    out_ref[...] = acc
    for copy in ys:
        copy.wait_send()
    for copy in zs:
        copy.wait_send()


def dp_scatter(x, step, collective_id):
    count, rows, width = x.shape
    columns = count // 2
    dma = pltpu.SemaphoreType.DMA
    return pl.pallas_call(
        lambda *refs: dp_scatter_kernel(step, *refs),
        out_shape=jax.ShapeDtypeStruct((rows, width), jnp.float32),
        in_specs=[VM],
        out_specs=VM,
        scratch_shapes=[
            pltpu.VMEM((columns, rows, width), x.dtype),
            pltpu.VMEM((columns - 1, rows, width), x.dtype),
            pltpu.VMEM((columns - 1, rows, width), x.dtype),
            dma((columns,)),
            dma((columns,)),
            dma((columns - 1,)),
            dma((columns - 1,)),
        ],
        compiler_params=pltpu.CompilerParams(collective_id=collective_id, has_side_effects=True),
        name="dp_scatter",
    )(x)


def per_device(tokens, cotangent, params, first_moment, second_moment):
    zero_count = lax.axis_size("zero")
    dp_count = lax.axis_size("dp")
    shard_size = params.shape[2]
    quarter = D // zero_count
    ff_part = FF // zero_count
    ffn_piece = 3 * D * FF // zero_count // dp_count
    attn_piece = shard_size - ffn_piece
    attn_rows, attn_step = attn_piece // D, attn_piece % D
    aligned = ffn_piece % D == 0 and attn_rows % 16 == 0 and dp_count == 8
    lift_end = 2 * ff_part * D
    first_end = 3 * quarter * D
    second_end = first_end + D * quarter
    if aligned:
        own = params.reshape(shard_size)
        ffn_own = own[:ffn_piece].reshape(ffn_piece // D, D).astype(jnp.bfloat16)
        pad_rows = attn_rows + 8
        attn_own = jnp.pad(own[ffn_piece:], (0, pad_rows * D - attn_piece)).reshape(pad_rows, D)
        attn_own = shift_piece(attn_own, attn_step, attn_rows + 16)
        attn_all, gain_rows, cot_full = dp_gather(
            attn_own, cotangent.reshape(-1, D), attn_rows, 1
        )
        ffn_own, attn_all = lax.optimization_barrier((ffn_own, attn_all))
        ffn_all = lax.all_gather(ffn_own, "dp", axis=0, tiled=True)
        edge = jnp.concatenate([jnp.zeros((1, D), jnp.bfloat16), attn_all[:-1, attn_rows]])
        body = attn_all[:, :attn_rows]
        lead = lax.broadcasted_iota(jnp.int32, body.shape, 1) == 0
        body = body + jnp.where(lead, edge[:, None, :], jnp.zeros((), jnp.bfloat16))
        body = body.reshape(dp_count * attn_rows, D)
        w_qkv = body[: 3 * quarter]
        w_attn = body[3 * quarter :].reshape(D, quarter)
        gains = gain_rows[:, 0, : 2 * quarter].reshape(zero_count, 2, quarter)
        gains = jnp.transpose(gains, (1, 0, 2)).reshape(2, D)
        w_input = ffn_all[: 2 * ff_part]
        w_output = ffn_all[2 * ff_part :].reshape(D, ff_part)
    else:
        own_bf = params.astype(jnp.bfloat16)
        slice_all = lax.all_gather(own_bf, "dp", axis=1, tiled=True).reshape(dp_count, shard_size)
        ffn_flat = slice_all[:, :ffn_piece].reshape(-1)
        attn_flat = slice_all[:, ffn_piece:].reshape(-1)
        w_qkv = attn_flat[:first_end].reshape(3 * quarter, D)
        w_attn = attn_flat[first_end:second_end].reshape(D, quarter)
        gains = lax.all_gather(
            attn_flat[second_end:].reshape(2, quarter), "zero", axis=1, tiled=True
        )
        w_input = ffn_flat[:lift_end].reshape(2 * ff_part, D)
        w_output = ffn_flat[lift_end:].reshape(D, ff_part)
    gain_one32 = gains[0].astype(jnp.float32)
    gain_two32 = gains[1].astype(jnp.float32)
    seq_count, own_len = (tokens.shape[0], tokens.shape[1])
    own_rows = seq_count * own_len
    length = own_len * zero_count
    row_count = seq_count * length
    local_heads = quarter // HEAD
    block_rows = 2 * HALF_WIN
    block_count = length // block_rows
    cosine, sine_table = rotary_tables(length)
    allowed = band_mask(length, block_rows)[None, :, None]
    inputs = tokens.astype(jnp.float32).reshape(own_rows, D)
    normed_one, inverse_one = norm_forward(inputs)
    normal_one = (normed_one * gain_one32).astype(jnp.bfloat16).reshape(seq_count, own_len, D)
    full_one = zero_gather(normal_one.reshape(own_rows, D), 2)
    projected = jnp.dot(full_one, w_qkv.T, preferred_element_type=jnp.float32)
    projected = projected.reshape(seq_count, length, 3, local_heads, HEAD)
    queries = (projected[:, :, 0] * cosine + rotate_half(projected[:, :, 0]) * sine_table).astype(
        jnp.bfloat16
    )
    key_rows = (projected[:, :, 1] * cosine + rotate_half(projected[:, :, 1]) * sine_table).astype(
        jnp.bfloat16
    )
    value_rows = projected[:, :, 2].astype(jnp.bfloat16)
    query_blocks = queries.reshape(seq_count, block_count, block_rows, local_heads, HEAD)
    key_windows = window_keys(key_rows, block_rows)
    value_windows = window_keys(value_rows, block_rows)
    scores = (
        jnp.einsum(
            "sbqhe,sbkhe->sbhqk", query_blocks, key_windows, preferred_element_type=jnp.float32
        )
        * 0.125
    )
    scores = jnp.where(allowed, scores, masked_score)
    row_max = jnp.max(scores, axis=-1, keepdims=True)
    log_total = row_max + jnp.log(jnp.sum(jnp.exp(scores - row_max), axis=-1, keepdims=True))
    attn_probs = jnp.exp(scores - log_total).astype(jnp.bfloat16)
    context = jnp.einsum(
        "sbhqk,sbkhe->sbqhe", attn_probs, value_windows, preferred_element_type=jnp.float32
    ).astype(jnp.bfloat16)
    context_rows = context.reshape(row_count, quarter)
    attn_terms = jnp.dot(context_rows, w_attn.T, preferred_element_type=jnp.float32)
    attn_sum = zero_scatter(attn_terms.astype(jnp.bfloat16), 6)
    hidden = inputs + attn_sum.reshape(own_rows, D)
    normed_two, inverse_two = norm_forward(hidden)
    normal_two = (normed_two * gain_two32).astype(jnp.bfloat16).reshape(seq_count, own_len, D)
    full_two = zero_gather(normal_two.reshape(own_rows, D), 3)
    lifted = jnp.dot(full_two, w_input.T, preferred_element_type=jnp.float32)
    gate_act, gate_slope = gelu_parts(lifted[:, :ff_part])
    up_half = lifted[:, ff_part:]
    mixed = (gate_act * up_half).astype(jnp.bfloat16)
    ffn_terms = jnp.dot(mixed, w_output.T, preferred_element_type=jnp.float32)
    ffn_sum = lax.psum_scatter(
        ffn_terms.astype(jnp.bfloat16), "zero", scatter_dimension=0, tiled=True
    )
    grad_scale = float(dp_count * row_count) ** (-0.5)
    if not aligned:
        cot_full = lax.all_gather(cotangent, "zero", axis=1, tiled=True)
    cot_full = cot_full.reshape(row_count, D)
    grad_output_w = jnp.dot(cot_full.T, mixed, preferred_element_type=jnp.float32)
    grad_mixed = jnp.dot(cot_full, w_output, preferred_element_type=jnp.float32)
    grad_lifted = jnp.concatenate(
        [grad_mixed * up_half * gate_slope, grad_mixed * gate_act], axis=-1
    ).astype(jnp.bfloat16)
    grad_input_w = jnp.dot(grad_lifted.T, full_two, preferred_element_type=jnp.float32)
    if aligned:
        ffn_grads = jnp.concatenate([grad_input_w, grad_output_w.reshape(ff_part, D)]) * grad_scale
        ffn_rows = ffn_piece // D
        ffn_pad = -ffn_rows % 16
        ffn_grads = ffn_grads.astype(jnp.bfloat16).reshape(dp_count, ffn_rows, D)
        ffn_grads = jnp.pad(ffn_grads, ((0, 0), (0, ffn_pad), (0, 0)))
        ffn_grads, grad_lifted = lax.optimization_barrier((ffn_grads, grad_lifted))
        ffn_shard = lax.psum_scatter(
            ffn_grads.reshape(dp_count * (ffn_rows + ffn_pad), D),
            "dp",
            scatter_dimension=0,
            tiled=True,
        )[:ffn_rows].astype(jnp.float32)
    else:
        ffn_vec = jnp.concatenate([grad_input_w.ravel(), grad_output_w.ravel()]) * grad_scale
        ffn_vec = ffn_vec.reshape(dp_count, ffn_piece)
    norm_two_terms = jnp.dot(grad_lifted, w_input, preferred_element_type=jnp.float32)
    grad_norm_two = zero_scatter(norm_two_terms.astype(jnp.bfloat16), 8)
    gain_two_term = jnp.sum(grad_norm_two * normed_two, axis=0)
    grad_hidden = cotangent.reshape(own_rows, D).astype(jnp.float32) + norm_backward(
        grad_norm_two, gain_two32, normed_two, inverse_two
    )
    grad_hidden_b = grad_hidden.astype(jnp.bfloat16).reshape(seq_count, own_len, D)
    hidden_full = zero_gather(grad_hidden_b.reshape(own_rows, D), 5)
    grad_attn_w = jnp.dot(hidden_full.T, context_rows, preferred_element_type=jnp.float32)
    grad_context = jnp.dot(hidden_full, w_attn, preferred_element_type=jnp.float32).astype(
        jnp.bfloat16
    )
    grad_context = grad_context.reshape(seq_count, block_count, block_rows, local_heads, HEAD)
    again = (
        jnp.einsum(
            "sbqhe,sbkhe->sbhqk", query_blocks, key_windows, preferred_element_type=jnp.float32
        )
        * 0.125
    )
    probs_full = jnp.exp(jnp.where(allowed, again, masked_score) - log_total)
    grad_probs = jnp.einsum(
        "sbqhe,sbkhe->sbhqk", grad_context, value_windows, preferred_element_type=jnp.float32
    )
    row_term = jnp.sum(grad_context.astype(jnp.float32) * context.astype(jnp.float32), axis=-1)
    row_term = jnp.transpose(row_term, (0, 1, 3, 2))[..., None]
    grad_scores = (probs_full * (grad_probs - row_term) * 0.125).astype(jnp.bfloat16)
    probs_b = probs_full.astype(jnp.bfloat16)
    grad_query = jnp.einsum(
        "sbhqk,sbkhe->sbqhe", grad_scores, key_windows, preferred_element_type=jnp.float32
    ).reshape(seq_count, length, local_heads, HEAD)
    grad_key = fold_keys(
        jnp.einsum(
            "sbhqk,sbqhe->sbkhe", grad_scores, query_blocks, preferred_element_type=jnp.float32
        ),
        block_rows,
    )
    grad_value = fold_keys(
        jnp.einsum("sbhqk,sbqhe->sbkhe", probs_b, grad_context, preferred_element_type=jnp.float32),
        block_rows,
    )
    grad_query = grad_query * cosine + rotate_back(grad_query * sine_table)
    grad_key = grad_key * cosine + rotate_back(grad_key * sine_table)
    grad_packed = (
        jnp.stack([grad_query, grad_key, grad_value], axis=2)
        .astype(jnp.bfloat16)
        .reshape(row_count, 3 * quarter)
    )
    grad_qkv_w = jnp.dot(grad_packed.T, full_one, preferred_element_type=jnp.float32)
    norm_one_terms = jnp.dot(grad_packed, w_qkv, preferred_element_type=jnp.float32)
    grad_norm_one, gain_sums = zero_scatter_gain(
        norm_one_terms.astype(jnp.bfloat16), normed_one, gain_two_term[None], 9
    )
    ffn_sum, gain_sums = lax.optimization_barrier((ffn_sum, gain_sums))
    output = hidden + ffn_sum.astype(jnp.float32)
    grad_inputs = grad_hidden + norm_backward(grad_norm_one, gain_one32, normed_one, inverse_one)
    gain_grads = lax.dynamic_slice(
        gain_sums, (0, lax.axis_index("zero") * quarter), (2, quarter)
    )
    if aligned:
        gain_row = jnp.pad(gain_grads.reshape(1, 2 * quarter), ((0, 0), (0, D - 2 * quarter)))
        grad_rows = jnp.concatenate([grad_qkv_w, grad_attn_w.reshape(quarter, D), gain_row])
        grad_rows = (grad_rows * grad_scale).astype(jnp.bfloat16)
        chunks = grad_rows[:-1].reshape(dp_count, attn_rows, D)
        chunks = jnp.concatenate(
            [
                chunks,
                jnp.concatenate([chunks[1:, :1], grad_rows[-1:][None]]),
                jnp.zeros((dp_count, 15, D), jnp.bfloat16),
            ],
            axis=1,
        )
        attn_shard = dp_scatter(chunks, attn_step, 10).reshape(-1)[:attn_piece]
        grad_shard = jnp.concatenate([ffn_shard.reshape(-1), attn_shard])
    else:
        attn_vec = (
            jnp.concatenate([grad_qkv_w.ravel(), grad_attn_w.ravel(), gain_grads.ravel()])
            * grad_scale
        )
        attn_vec = attn_vec.reshape(dp_count, attn_piece)
        grad_shard = lax.psum_scatter(
            jnp.concatenate([ffn_vec, attn_vec], axis=1), "dp", scatter_dimension=0, tiled=True
        )
    grad_shard = grad_shard.reshape(params.shape)
    new_first = beta_one * first_moment + (1.0 - beta_one) * grad_shard
    new_second = beta_two * second_moment + (1.0 - beta_two) * grad_shard * grad_shard
    first_hat = new_first / (1.0 - beta_one**STEP)
    second_hat = new_second / (1.0 - beta_two**STEP)
    attn_total = attn_piece * dp_count
    place = lax.axis_index("dp") * attn_piece + lax.iota(jnp.int32, attn_piece)
    gain_tail = place >= attn_total - 2 * quarter
    gain_part = jnp.concatenate([jnp.zeros((ffn_piece,), jnp.bool_), gain_tail]).reshape(
        params.shape
    )
    step_rate = jnp.where(gain_part, gain_rate, matrix_rate)
    decay_rate = jnp.where(gain_part, 0.0, matrix_decay)
    direction = first_hat / (jnp.sqrt(second_hat) + adam_eps)
    new_params = params - step_rate * (direction + decay_rate * params)
    return (
        output.astype(jnp.bfloat16).reshape(tokens.shape),
        grad_inputs.reshape(tokens.shape),
        grad_shard,
        new_params,
        new_first,
        new_second,
    )


def solution(mesh):
    in_specs = (
        P("dp", "zero", None),
        P("dp", "zero", None),
        P("zero", "dp", None),
        P("zero", "dp", None),
        P("zero", "dp", None),
    )
    out_specs = (
        P("dp", "zero", None),
        P("dp", "zero", None),
        P("zero", "dp", None),
        P("zero", "dp", None),
        P("zero", "dp", None),
        P("zero", "dp", None),
    )
    return jax.shard_map(
        per_device, mesh=mesh, in_specs=in_specs, out_specs=out_specs, check_vma=False
    )
```

```python
import math

import jax
import jax.numpy as jnp
from jax import lax
from jax.experimental import pallas as pl
from jax.experimental.pallas import tpu as pltpu
from jax.sharding import PartitionSpec as P


D = 768
FF = 1152
HEAD = 64
HALF_WIN = 64
STEP = 3


norm_eps = 1e-05
beta_one = 0.9
beta_two = 0.98
adam_eps = 1e-06
rope_base = 10000.0
matrix_rate = 0.01
matrix_decay = 0.1
gain_rate = 0.1
masked_score = -1e30


def norm_forward(values):
    centred = values - jnp.mean(values, axis=-1, keepdims=True)
    inverse = lax.rsqrt(jnp.mean(centred * centred, axis=-1, keepdims=True) + norm_eps)
    return (centred * inverse, inverse)


def norm_backward(grad_norm, gain_vec, normed, inverse):
    scaled = grad_norm * gain_vec
    return inverse * (
        scaled
        - jnp.mean(scaled, axis=-1, keepdims=True)
        - normed * jnp.mean(scaled * normed, axis=-1, keepdims=True)
    )


def rotary_tables(length):
    position = lax.iota(jnp.float32, length)
    exponent = lax.iota(jnp.float32, HEAD // 2) * (2.0 / HEAD)
    inv_freq = jnp.exp(-math.log(rope_base) * exponent)
    phases = position[:, None] * inv_freq[None, :]
    cosine = jnp.concatenate([jnp.cos(phases), jnp.cos(phases)], axis=-1)[:, None, :]
    sine_table = jnp.concatenate([jnp.sin(phases), jnp.sin(phases)], axis=-1)[:, None, :]
    return (cosine, sine_table)


def rotate_half(values):
    middle = values.shape[-1] // 2
    return jnp.concatenate([-values[..., middle:], values[..., :middle]], axis=-1)


def rotate_back(values):
    middle = values.shape[-1] // 2
    return jnp.concatenate([values[..., middle:], -values[..., :middle]], axis=-1)


def gelu_parts(values):
    cdf_part = 0.5 * (1.0 + jax.scipy.special.erf(values * (1.0 / math.sqrt(2.0))))
    pdf_part = jnp.exp(-0.5 * values * values) * (1.0 / math.sqrt(2.0 * math.pi))
    return (values * cdf_part, cdf_part + values * pdf_part)


def window_keys(values, block_rows):
    seq_count, length = (values.shape[0], values.shape[1])
    padded = jnp.pad(values, ((0, 0), (block_rows // 2, block_rows // 2), (0, 0), (0, 0)))
    blocks = padded.reshape(
        seq_count, length // block_rows + 1, block_rows, values.shape[2], values.shape[3]
    )
    return jnp.concatenate([blocks[:, :-1], blocks[:, 1:]], axis=2)


def fold_keys(windows, block_rows):
    seq_count, block_count = (windows.shape[0], windows.shape[1])
    zeros_block = jnp.zeros_like(windows[:, :1, :block_rows])
    low_part = jnp.concatenate([windows[:, :, :block_rows], zeros_block], axis=1)
    high_part = jnp.concatenate([zeros_block, windows[:, :, block_rows:]], axis=1)
    merged = (low_part + high_part).reshape(
        seq_count, (block_count + 1) * block_rows, windows.shape[3], windows.shape[4]
    )
    return merged[:, block_rows // 2 : block_rows // 2 + block_count * block_rows]


def band_mask(length, block_rows):
    block_count = length // block_rows
    dims = (block_count, block_rows, 2 * block_rows)
    query_pos = lax.broadcasted_iota(jnp.int32, dims, 1)
    key_pos = lax.broadcasted_iota(jnp.int32, dims, 2)
    block_pos = lax.broadcasted_iota(jnp.int32, dims, 0)
    relative = key_pos - query_pos
    absolute = block_pos * block_rows - block_rows // 2 + key_pos
    return (relative >= 0) & (relative <= block_rows) & (absolute >= 0) & (absolute < length)


MESH = pl.DeviceIdType.MESH
VM = pl.BlockSpec(memory_space=pltpu.VMEM)
PIECES = 4


def remote(src, dst, send_sem, recv_sem, axis, index):
    return pltpu.make_async_remote_copy(
        src_ref=src,
        dst_ref=dst,
        send_sem=send_sem,
        recv_sem=recv_sem,
        device_id={axis: index},
        device_id_type=MESH,
    )


def greet(targets):
    barrier = pltpu.get_barrier_semaphore()
    for axis, index in targets:
        pl.semaphore_signal(barrier, inc=1, device_id={axis: index}, device_id_type=MESH)
    pl.semaphore_wait(barrier, len(targets))


def zero_places():
    me = lax.axis_index("zero")
    chip, core = me // 2, me % 2
    mate = chip * 2 + 1 - core
    across = (1 - chip) * 2 + core
    diagonal = (1 - chip) * 2 + 1 - core
    return me, mate, across, diagonal


def zero_gather_kernel(x_ref, out_ref, own_sem, send_sem, recv_sem, far_send, far_recv, fwd_send, fwd_recv):
    me, mate, across, diagonal = zero_places()
    rows = x_ref.shape[0]
    part = rows // PIECES
    greet([("zero", mate), ("zero", across)])
    far, fwd = [], []
    for k in range(PIECES):
        copy = remote(
            x_ref.at[pl.ds(k * part, part)],
            out_ref.at[me, pl.ds(k * part, part)],
            far_send.at[k],
            far_recv.at[k],
            "zero",
            across,
        )
        copy.start()
        far.append(copy)
    near = remote(x_ref, out_ref.at[me], send_sem, recv_sem, "zero", mate)
    near.start()
    own = pltpu.make_async_copy(x_ref, out_ref.at[me], own_sem)
    own.start()
    for k in range(PIECES):
        far[k].wait_recv()
        piece = out_ref.at[across, pl.ds(k * part, part)]
        copy = remote(piece, piece, fwd_send.at[k], fwd_recv.at[k], "zero", mate)
        copy.start()
        fwd.append(copy)
    own.wait()
    near.wait()
    for k in range(PIECES):
        far[k].wait_send()
        fwd[k].wait()


def zero_gather(x, collective_id):
    zero_count = lax.axis_size("zero")
    rows, width = x.shape
    out = pl.pallas_call(
        zero_gather_kernel,
        out_shape=jax.ShapeDtypeStruct((zero_count, rows, width), x.dtype),
        in_specs=[VM],
        out_specs=VM,
        scratch_shapes=[pltpu.SemaphoreType.DMA] * 3 + [pltpu.SemaphoreType.DMA((PIECES,))] * 4,
        compiler_params=pltpu.CompilerParams(collective_id=collective_id, has_side_effects=True),
    )(x)
    return out.reshape(zero_count * rows, width)


def zero_scatter_parts(
    terms_ref, out_ref, mine, mixed, total, far, mate_send, mate_recv, mix_send, mix_recv, far_send, far_recv
):
    me, mate, across, diagonal = zero_places()
    part = terms_ref.shape[1] // PIECES
    near = remote(terms_ref.at[mate], mine, mate_send, mate_recv, "zero", mate)
    mixes, fars = [], []
    for k in range(PIECES):
        piece = pl.ds(k * part, part)
        mixes.append(
            remote(
                terms_ref.at[diagonal, piece],
                mixed.at[piece],
                mix_send.at[k],
                mix_recv.at[k],
                "zero",
                mate,
            )
        )
        fars.append(
            remote(
                total.at[piece], far.at[piece], far_send.at[k], far_recv.at[k], "zero", across
            )
        )

    def start():
        for copy in mixes:
            copy.start()
        near.start()
        for k in range(PIECES):
            mixes[k].wait_recv()
            piece = pl.ds(k * part, part)
            total[piece] = (
                terms_ref[across, piece].astype(jnp.float32) + mixed[piece].astype(jnp.float32)
            ).astype(jnp.bfloat16)
            fars[k].start()

    def finish():
        near.wait()
        for k in range(PIECES):
            piece = pl.ds(k * part, part)
            fars[k].wait_recv()
            out_ref[piece] = (
                terms_ref[me, piece].astype(jnp.float32)
                + mine[piece].astype(jnp.float32)
                + far[piece].astype(jnp.float32)
            )
        for k in range(PIECES):
            mixes[k].wait_send()
            fars[k].wait_send()

    return start, finish


def zero_scatter_kernel(terms_ref, out_ref, *rest, extra=False):
    me, mate, across, diagonal = zero_places()
    greet([("zero", mate), ("zero", across)] + [("zero", diagonal)] * extra)
    start, finish = zero_scatter_parts(terms_ref, out_ref, *rest)
    start()
    finish()


def zero_scatter(terms, collective_id):
    zero_count = lax.axis_size("zero")
    rows, width = terms.shape[0] // zero_count, terms.shape[1]
    buf = pltpu.VMEM((rows, width), jnp.bfloat16)
    return pl.pallas_call(
        zero_scatter_kernel,
        out_shape=jax.ShapeDtypeStruct((rows, width), jnp.float32),
        in_specs=[VM],
        out_specs=VM,
        scratch_shapes=[buf] * 4
        + [pltpu.SemaphoreType.DMA] * 2
        + [pltpu.SemaphoreType.DMA((PIECES,))] * 4,
        compiler_params=pltpu.CompilerParams(collective_id=collective_id, has_side_effects=True),
    )(terms.reshape(zero_count, rows, width))


def zero_scatter_gain_kernel(
    terms_ref,
    normed_ref,
    other_ref,
    out_ref,
    gain_ref,
    mine,
    mixed,
    total,
    far,
    gain_own,
    gain_in,
    mate_send,
    mate_recv,
    gain_send,
    gain_recv,
    *sems,
):
    me, mate, across, diagonal = zero_places()
    zero_scatter_kernel(
        terms_ref, out_ref, mine, mixed, total, far, mate_send, mate_recv, *sems, extra=True
    )
    gain_own[...] = jnp.zeros_like(gain_own)
    gain_own[pl.ds(0, 1)] = jnp.sum(out_ref[...] * normed_ref[...], axis=0, keepdims=True)
    gain_own[pl.ds(1, 1)] = other_ref[...]
    copies = []
    for k, index in enumerate((mate, across, diagonal)):
        copy = remote(gain_own, gain_in.at[k], gain_send.at[k], gain_recv.at[k], "zero", index)
        copy.start()
        copies.append(copy)
    total_gain = gain_own[...]
    for k, copy in enumerate(copies):
        copy.wait()
        total_gain = total_gain + gain_in[k]
    gain_ref[...] = total_gain


def zero_scatter_gain(terms, normed, other, collective_id):
    zero_count = lax.axis_size("zero")
    rows, width = terms.shape[0] // zero_count, terms.shape[1]
    buf = pltpu.VMEM((rows, width), jnp.bfloat16)
    dma = pltpu.SemaphoreType.DMA
    return pl.pallas_call(
        zero_scatter_gain_kernel,
        out_shape=(
            jax.ShapeDtypeStruct((rows, width), jnp.float32),
            jax.ShapeDtypeStruct((8, width), jnp.float32),
        ),
        in_specs=[VM] * 3,
        out_specs=(VM, VM),
        scratch_shapes=[buf] * 4
        + [pltpu.VMEM((8, width), jnp.float32), pltpu.VMEM((3, 8, width), jnp.float32)]
        + [dma] * 2
        + [dma((3,))] * 2
        + [dma((PIECES,))] * 4,
        compiler_params=pltpu.CompilerParams(collective_id=collective_id, has_side_effects=True),
    )(terms.reshape(zero_count, rows, width), normed, other)


def shift_kernel(step, x_ref, out_ref):
    x = x_ref[...]
    rows, width = x.shape
    shift = lax.axis_index("dp") * step
    rolled = pltpu.roll(x, shift, axis=1)
    above = pltpu.roll(rolled, 1, axis=0)
    lane = lax.broadcasted_iota(jnp.int32, x.shape, 1)
    out_ref[pl.ds(0, rows)] = jnp.where(lane >= shift, rolled, above).astype(out_ref.dtype)
    if out_ref.shape[0] > rows:
        out_ref[pl.ds(rows, out_ref.shape[0] - rows)] = jnp.zeros(
            (out_ref.shape[0] - rows, width), out_ref.dtype
        )


def shift_piece(x, step, out_rows):
    return pl.pallas_call(
        lambda *refs: shift_kernel(step, *refs),
        out_shape=jax.ShapeDtypeStruct((out_rows, x.shape[1]), jnp.bfloat16),
        in_specs=[VM],
        out_specs=VM,
        name="shift_piece",
    )(x)


def dp_gather_kernel(
    tail,
    x_ref,
    cot_ref,
    out_ref,
    gains_ref,
    cots_ref,
    own_sem,
    own_gain,
    own_cot,
    up_send,
    up_recv,
    down_send,
    down_recv,
    y_send,
    y_recv,
    g_send,
    g_recv,
    c_send,
    c_recv,
):
    me = lax.axis_index("dp")
    count = out_ref.shape[0]
    columns = count // 2
    z_me, y_me = me // 2, me % 2
    peer = z_me * 2 + 1 - y_me
    above, below = z_me < columns - 1, z_me > 0
    zero_me = lax.axis_index("zero")
    zero_count = gains_ref.shape[0]
    others = [lax.rem(zero_me + k, zero_count) for k in range(1, zero_count)]
    barrier = pltpu.get_barrier_semaphore()

    def hello(axis, index):
        pl.semaphore_signal(barrier, inc=1, device_id={axis: index}, device_id_type=MESH)

    hello("dp", peer)
    for index in others:
        hello("zero", index)
    pl.when(above)(lambda: hello("dp", me + 2))
    pl.when(below)(lambda: hello("dp", me - 2))
    ends = (z_me == 0).astype(jnp.int32) + (z_me == columns - 1).astype(jnp.int32)
    pl.semaphore_wait(barrier, zero_count + 2 - ends)

    def up(k, src):
        piece = out_ref.at[me - 2 * k]
        return remote(piece if src is None else src, piece, up_send.at[k], up_recv.at[k + 1], "dp", me + 2)

    def down(k, src):
        piece = out_ref.at[me + 2 * k]
        return remote(piece if src is None else src, piece, down_send.at[k], down_recv.at[k + 1], "dp", me - 2)

    def side(z, src):
        piece = out_ref.at[z * 2 + y_me]
        return remote(piece if src is None else src, piece, y_send.at[z], y_recv.at[z], "dp", peer)

    def arrive(k, rising):
        make, sems = (up, up_recv) if rising else (down, down_recv)
        source = z_me - k if rising else z_me + k
        piece = out_ref.at[source * 2 + y_me]
        remote(piece, piece, own_gain, sems.at[k], "dp", peer).wait_recv()
        if k < columns - 1:
            pl.when(above if rising else below)(lambda: make(k, None).start())
        side(source, None).start()

    pl.when(above)(lambda: up(0, x_ref).start())
    pl.when(below)(lambda: down(0, x_ref).start())
    side(z_me, x_ref).start()
    own = pltpu.make_async_copy(x_ref, out_ref.at[me], own_sem)
    own.start()
    own_c = pltpu.make_async_copy(cot_ref, cots_ref.at[zero_me], own_cot)
    own_c.start()
    cs = []
    for k in range(zero_count - 1):
        copy = remote(cot_ref, cots_ref.at[zero_me], c_send.at[k], c_recv.at[k], "zero", others[k])
        copy.start()
        cs.append(copy)
    for k in range(1, columns):
        pl.when(z_me >= k)(lambda: arrive(k, True))
        pl.when(z_me + k < columns)(lambda: arrive(k, False))
    own.wait()
    for z in range(columns):
        side(z, None).wait()
    last = out_ref.at[count - 1, pl.ds(tail, 16)]
    own = pltpu.make_async_copy(last, gains_ref.at[zero_me], own_gain)
    own.start()
    gs = []
    for k in range(zero_count - 1):
        copy = remote(last, gains_ref.at[zero_me], g_send.at[k], g_recv.at[k], "zero", others[k])
        copy.start()
        gs.append(copy)
    own.wait()
    for copy in gs:
        copy.wait()
    own_c.wait()
    for copy in cs:
        copy.wait()
    for k in range(columns - 1):
        pl.when(above & (z_me >= k))(lambda: up(k, None).wait_send())
        pl.when(below & (z_me + k < columns))(lambda: down(k, None).wait_send())


def dp_gather(x, cot, tail, collective_id):
    count, zero_count = lax.axis_size("dp"), lax.axis_size("zero")
    columns = count // 2
    rows, width = x.shape
    dma = pltpu.SemaphoreType.DMA
    return pl.pallas_call(
        lambda *refs: dp_gather_kernel(tail, *refs),
        out_shape=(
            jax.ShapeDtypeStruct((count, rows, width), x.dtype),
            jax.ShapeDtypeStruct((zero_count, 16, width), x.dtype),
            jax.ShapeDtypeStruct((zero_count, *cot.shape), cot.dtype),
        ),
        in_specs=[VM, VM],
        out_specs=(VM, VM, VM),
        scratch_shapes=[
            dma,
            dma,
            dma,
            *[dma((columns,))] * 6,
            *[dma((zero_count - 1,))] * 4,
        ],
        compiler_params=pltpu.CompilerParams(collective_id=collective_id, has_side_effects=True),
        name="dp_gather",
    )(x, cot)


def dp_scatter_kernel(
    step,
    x_ref,
    terms_ref,
    out_ref,
    sum_ref,
    pair,
    total,
    far,
    y_send,
    y_recv,
    z_send,
    z_recv,
    *rest,
):
    start_zero, finish_zero = zero_scatter_parts(terms_ref, sum_ref, *rest)
    me = lax.axis_index("dp")
    count, rows, width = x_ref.shape
    columns = count // 2
    z_me, y_me = me // 2, me % 2
    peer = z_me * 2 + 1 - y_me
    order = [lax.rem(z_me + k, columns) for k in (*range(1, columns), 0)]
    zero_me, mate, across, diagonal = zero_places()
    greet(
        [("dp", peer)]
        + [("dp", z * 2 + y_me) for z in order[:-1]]
        + [("zero", mate), ("zero", across)]
    )
    ys, zs = [], []
    for k in range(columns):
        copy = remote(
            x_ref.at[order[k] * 2 + 1 - y_me], pair.at[k], y_send.at[k], y_recv.at[k], "dp", peer
        )
        copy.start()
        ys.append(copy)
    start_zero()
    for k in range(columns - 1):
        ys[k].wait_recv()
        total[k] = (
            x_ref[order[k] * 2 + y_me].astype(jnp.float32) + pair[k].astype(jnp.float32)
        ).astype(jnp.bfloat16)
        copy = remote(
            total.at[k], far.at[k], z_send.at[k], z_recv.at[k], "dp", order[k] * 2 + y_me
        )
        copy.start()
        zs.append(copy)
    finish_zero()
    ys[columns - 1].wait_recv()
    acc = x_ref[me].astype(jnp.float32) + pair[columns - 1].astype(jnp.float32)
    for k in range(columns - 1):
        zs[k].wait_recv()
        acc = acc + far[k].astype(jnp.float32)
    if step:
        shift = me * step
        rolled = pltpu.roll(acc, lax.rem(width - shift, width), axis=1)
        below = pltpu.roll(rolled, rows - 1, axis=0)
        lane = lax.broadcasted_iota(jnp.int32, acc.shape, 1)
        acc = jnp.where(lane + shift < width, rolled, below)
    out_ref[...] = acc
    for copy in ys:
        copy.wait_send()
    for copy in zs:
        copy.wait_send()


def dp_scatter(x, terms, step, collective_id):
    count, rows, width = x.shape
    zero_count = lax.axis_size("zero")
    own_rows = terms.shape[0] // zero_count
    buf = pltpu.VMEM((own_rows, width), terms.dtype)
    columns = count // 2
    dma = pltpu.SemaphoreType.DMA
    return pl.pallas_call(
        lambda *refs: dp_scatter_kernel(step, *refs),
        out_shape=(
            jax.ShapeDtypeStruct((rows, width), jnp.float32),
            jax.ShapeDtypeStruct((own_rows, width), jnp.float32),
        ),
        in_specs=[VM, VM],
        out_specs=(VM, VM),
        scratch_shapes=[
            pltpu.VMEM((columns, rows, width), x.dtype),
            pltpu.VMEM((columns - 1, rows, width), x.dtype),
            pltpu.VMEM((columns - 1, rows, width), x.dtype),
            dma((columns,)),
            dma((columns,)),
            dma((columns - 1,)),
            dma((columns - 1,)),
        ]
        + [buf] * 4
        + [dma] * 2
        + [dma((PIECES,))] * 4,
        compiler_params=pltpu.CompilerParams(collective_id=collective_id, has_side_effects=True),
        name="dp_scatter",
    )(x, terms.reshape(zero_count, own_rows, width))


def per_device(tokens, cotangent, params, first_moment, second_moment):
    zero_count = lax.axis_size("zero")
    dp_count = lax.axis_size("dp")
    shard_size = params.shape[2]
    quarter = D // zero_count
    ff_part = FF // zero_count
    ffn_piece = 3 * D * FF // zero_count // dp_count
    attn_piece = shard_size - ffn_piece
    attn_rows, attn_step = attn_piece // D, attn_piece % D
    aligned = ffn_piece % D == 0 and attn_rows % 16 == 0 and dp_count == 8
    lift_end = 2 * ff_part * D
    first_end = 3 * quarter * D
    second_end = first_end + D * quarter
    if aligned:
        own = params.reshape(shard_size)
        ffn_own = own[:ffn_piece].reshape(ffn_piece // D, D).astype(jnp.bfloat16)
        pad_rows = attn_rows + 8
        attn_own = jnp.pad(own[ffn_piece:], (0, pad_rows * D - attn_piece)).reshape(pad_rows, D)
        attn_own = shift_piece(attn_own, attn_step, attn_rows + 16)
        attn_all, gain_rows, cot_full = dp_gather(
            attn_own, cotangent.reshape(-1, D), attn_rows, 1
        )
        ffn_own, attn_all = lax.optimization_barrier((ffn_own, attn_all))
        ffn_all = lax.all_gather(ffn_own, "dp", axis=0, tiled=True)
        edge = jnp.concatenate([jnp.zeros((1, D), jnp.bfloat16), attn_all[:-1, attn_rows]])
        body = attn_all[:, :attn_rows]
        lead = lax.broadcasted_iota(jnp.int32, body.shape, 1) == 0
        body = body + jnp.where(lead, edge[:, None, :], jnp.zeros((), jnp.bfloat16))
        body = body.reshape(dp_count * attn_rows, D)
        w_qkv = body[: 3 * quarter]
        w_attn = body[3 * quarter :].reshape(D, quarter)
        gains = gain_rows[:, 0, : 2 * quarter].reshape(zero_count, 2, quarter)
        gains = jnp.transpose(gains, (1, 0, 2)).reshape(2, D)
        w_input = ffn_all[: 2 * ff_part]
        w_output = ffn_all[2 * ff_part :].reshape(D, ff_part)
    else:
        own_bf = params.astype(jnp.bfloat16)
        slice_all = lax.all_gather(own_bf, "dp", axis=1, tiled=True).reshape(dp_count, shard_size)
        ffn_flat = slice_all[:, :ffn_piece].reshape(-1)
        attn_flat = slice_all[:, ffn_piece:].reshape(-1)
        w_qkv = attn_flat[:first_end].reshape(3 * quarter, D)
        w_attn = attn_flat[first_end:second_end].reshape(D, quarter)
        gains = lax.all_gather(
            attn_flat[second_end:].reshape(2, quarter), "zero", axis=1, tiled=True
        )
        w_input = ffn_flat[:lift_end].reshape(2 * ff_part, D)
        w_output = ffn_flat[lift_end:].reshape(D, ff_part)
    gain_one32 = gains[0].astype(jnp.float32)
    gain_two32 = gains[1].astype(jnp.float32)
    seq_count, own_len = (tokens.shape[0], tokens.shape[1])
    own_rows = seq_count * own_len
    length = own_len * zero_count
    row_count = seq_count * length
    local_heads = quarter // HEAD
    block_rows = 2 * HALF_WIN
    block_count = length // block_rows
    cosine, sine_table = rotary_tables(length)
    allowed = band_mask(length, block_rows)[None, :, None]
    inputs = tokens.astype(jnp.float32).reshape(own_rows, D)
    normed_one, inverse_one = norm_forward(inputs)
    normal_one = (normed_one * gain_one32).astype(jnp.bfloat16).reshape(seq_count, own_len, D)
    full_one = zero_gather(normal_one.reshape(own_rows, D), 2)
    projected = jnp.dot(full_one, w_qkv.T, preferred_element_type=jnp.float32)
    projected = projected.reshape(seq_count, length, 3, local_heads, HEAD)
    queries = (projected[:, :, 0] * cosine + rotate_half(projected[:, :, 0]) * sine_table).astype(
        jnp.bfloat16
    )
    key_rows = (projected[:, :, 1] * cosine + rotate_half(projected[:, :, 1]) * sine_table).astype(
        jnp.bfloat16
    )
    value_rows = projected[:, :, 2].astype(jnp.bfloat16)
    query_blocks = queries.reshape(seq_count, block_count, block_rows, local_heads, HEAD)
    key_windows = window_keys(key_rows, block_rows)
    value_windows = window_keys(value_rows, block_rows)
    scores = (
        jnp.einsum(
            "sbqhe,sbkhe->sbhqk", query_blocks, key_windows, preferred_element_type=jnp.float32
        )
        * 0.125
    )
    scores = jnp.where(allowed, scores, masked_score)
    row_max = jnp.max(scores, axis=-1, keepdims=True)
    log_total = row_max + jnp.log(jnp.sum(jnp.exp(scores - row_max), axis=-1, keepdims=True))
    attn_probs = jnp.exp(scores - log_total).astype(jnp.bfloat16)
    context = jnp.einsum(
        "sbhqk,sbkhe->sbqhe", attn_probs, value_windows, preferred_element_type=jnp.float32
    ).astype(jnp.bfloat16)
    context_rows = context.reshape(row_count, quarter)
    attn_terms = jnp.dot(context_rows, w_attn.T, preferred_element_type=jnp.float32)
    attn_sum = zero_scatter(attn_terms.astype(jnp.bfloat16), 6)
    hidden = inputs + attn_sum.reshape(own_rows, D)
    normed_two, inverse_two = norm_forward(hidden)
    normal_two = (normed_two * gain_two32).astype(jnp.bfloat16).reshape(seq_count, own_len, D)
    full_two = zero_gather(normal_two.reshape(own_rows, D), 3)
    lifted = jnp.dot(full_two, w_input.T, preferred_element_type=jnp.float32)
    gate_act, gate_slope = gelu_parts(lifted[:, :ff_part])
    up_half = lifted[:, ff_part:]
    mixed = (gate_act * up_half).astype(jnp.bfloat16)
    ffn_terms = jnp.dot(mixed, w_output.T, preferred_element_type=jnp.float32)
    ffn_terms = ffn_terms.astype(jnp.bfloat16)
    grad_scale = float(dp_count * row_count) ** (-0.5)
    if not aligned:
        cot_full = lax.all_gather(cotangent, "zero", axis=1, tiled=True)
    cot_full = cot_full.reshape(row_count, D)
    grad_output_w = jnp.dot(cot_full.T, mixed, preferred_element_type=jnp.float32)
    grad_mixed = jnp.dot(cot_full, w_output, preferred_element_type=jnp.float32)
    grad_lifted = jnp.concatenate(
        [grad_mixed * up_half * gate_slope, grad_mixed * gate_act], axis=-1
    ).astype(jnp.bfloat16)
    grad_input_w = jnp.dot(grad_lifted.T, full_two, preferred_element_type=jnp.float32)
    if aligned:
        ffn_grads = jnp.concatenate([grad_input_w, grad_output_w.reshape(ff_part, D)]) * grad_scale
        ffn_rows = ffn_piece // D
        ffn_pad = -ffn_rows % 16
        ffn_grads = ffn_grads.astype(jnp.bfloat16).reshape(dp_count, ffn_rows, D)
        ffn_grads = jnp.pad(ffn_grads, ((0, 0), (0, ffn_pad), (0, 0)))
        ffn_grads, grad_lifted = lax.optimization_barrier((ffn_grads, grad_lifted))
        ffn_shard = lax.psum_scatter(
            ffn_grads.reshape(dp_count * (ffn_rows + ffn_pad), D),
            "dp",
            scatter_dimension=0,
            tiled=True,
        )[:ffn_rows].astype(jnp.float32)
    else:
        ffn_vec = jnp.concatenate([grad_input_w.ravel(), grad_output_w.ravel()]) * grad_scale
        ffn_vec = ffn_vec.reshape(dp_count, ffn_piece)
    norm_two_terms = jnp.dot(grad_lifted, w_input, preferred_element_type=jnp.float32)
    grad_norm_two = zero_scatter(norm_two_terms.astype(jnp.bfloat16), 8)
    gain_two_term = jnp.sum(grad_norm_two * normed_two, axis=0)
    grad_hidden = cotangent.reshape(own_rows, D).astype(jnp.float32) + norm_backward(
        grad_norm_two, gain_two32, normed_two, inverse_two
    )
    grad_hidden_b = grad_hidden.astype(jnp.bfloat16).reshape(seq_count, own_len, D)
    hidden_full = zero_gather(grad_hidden_b.reshape(own_rows, D), 5)
    grad_attn_w = jnp.dot(hidden_full.T, context_rows, preferred_element_type=jnp.float32)
    grad_context = jnp.dot(hidden_full, w_attn, preferred_element_type=jnp.float32).astype(
        jnp.bfloat16
    )
    grad_context = grad_context.reshape(seq_count, block_count, block_rows, local_heads, HEAD)
    again = (
        jnp.einsum(
            "sbqhe,sbkhe->sbhqk", query_blocks, key_windows, preferred_element_type=jnp.float32
        )
        * 0.125
    )
    probs_full = jnp.exp(jnp.where(allowed, again, masked_score) - log_total)
    grad_probs = jnp.einsum(
        "sbqhe,sbkhe->sbhqk", grad_context, value_windows, preferred_element_type=jnp.float32
    )
    row_term = jnp.sum(grad_context.astype(jnp.float32) * context.astype(jnp.float32), axis=-1)
    row_term = jnp.transpose(row_term, (0, 1, 3, 2))[..., None]
    grad_scores = (probs_full * (grad_probs - row_term) * 0.125).astype(jnp.bfloat16)
    probs_b = probs_full.astype(jnp.bfloat16)
    grad_query = jnp.einsum(
        "sbhqk,sbkhe->sbqhe", grad_scores, key_windows, preferred_element_type=jnp.float32
    ).reshape(seq_count, length, local_heads, HEAD)
    grad_key = fold_keys(
        jnp.einsum(
            "sbhqk,sbqhe->sbkhe", grad_scores, query_blocks, preferred_element_type=jnp.float32
        ),
        block_rows,
    )
    grad_value = fold_keys(
        jnp.einsum("sbhqk,sbqhe->sbkhe", probs_b, grad_context, preferred_element_type=jnp.float32),
        block_rows,
    )
    grad_query = grad_query * cosine + rotate_back(grad_query * sine_table)
    grad_key = grad_key * cosine + rotate_back(grad_key * sine_table)
    grad_packed = (
        jnp.stack([grad_query, grad_key, grad_value], axis=2)
        .astype(jnp.bfloat16)
        .reshape(row_count, 3 * quarter)
    )
    grad_qkv_w = jnp.dot(grad_packed.T, full_one, preferred_element_type=jnp.float32)
    norm_one_terms = jnp.dot(grad_packed, w_qkv, preferred_element_type=jnp.float32)
    grad_norm_one, gain_sums = zero_scatter_gain(
        norm_one_terms.astype(jnp.bfloat16), normed_one, gain_two_term[None], 9
    )
    grad_inputs = grad_hidden + norm_backward(grad_norm_one, gain_one32, normed_one, inverse_one)
    gain_grads = lax.dynamic_slice(
        gain_sums, (0, lax.axis_index("zero") * quarter), (2, quarter)
    )
    if aligned:
        gain_row = jnp.pad(gain_grads.reshape(1, 2 * quarter), ((0, 0), (0, D - 2 * quarter)))
        grad_rows = jnp.concatenate([grad_qkv_w, grad_attn_w.reshape(quarter, D), gain_row])
        grad_rows = (grad_rows * grad_scale).astype(jnp.bfloat16)
        chunks = grad_rows[:-1].reshape(dp_count, attn_rows, D)
        chunks = jnp.concatenate(
            [
                chunks,
                jnp.concatenate([chunks[1:, :1], grad_rows[-1:][None]]),
                jnp.zeros((dp_count, 15, D), jnp.bfloat16),
            ],
            axis=1,
        )
        attn_shard, ffn_sum = dp_scatter(chunks, ffn_terms, attn_step, 10)
        attn_shard = attn_shard.reshape(-1)[:attn_piece]
        grad_shard = jnp.concatenate([ffn_shard.reshape(-1), attn_shard])
    else:
        attn_vec = (
            jnp.concatenate([grad_qkv_w.ravel(), grad_attn_w.ravel(), gain_grads.ravel()])
            * grad_scale
        )
        attn_vec = attn_vec.reshape(dp_count, attn_piece)
        grad_shard = lax.psum_scatter(
            jnp.concatenate([ffn_vec, attn_vec], axis=1), "dp", scatter_dimension=0, tiled=True
        )
        ffn_sum = zero_scatter(ffn_terms, 7)
    output = hidden + ffn_sum
    grad_shard = grad_shard.reshape(params.shape)
    new_first = beta_one * first_moment + (1.0 - beta_one) * grad_shard
    new_second = beta_two * second_moment + (1.0 - beta_two) * grad_shard * grad_shard
    first_hat = new_first / (1.0 - beta_one**STEP)
    second_hat = new_second / (1.0 - beta_two**STEP)
    attn_total = attn_piece * dp_count
    place = lax.axis_index("dp") * attn_piece + lax.iota(jnp.int32, attn_piece)
    gain_tail = place >= attn_total - 2 * quarter
    gain_part = jnp.concatenate([jnp.zeros((ffn_piece,), jnp.bool_), gain_tail]).reshape(
        params.shape
    )
    step_rate = jnp.where(gain_part, gain_rate, matrix_rate)
    decay_rate = jnp.where(gain_part, 0.0, matrix_decay)
    direction = first_hat / (jnp.sqrt(second_hat) + adam_eps)
    new_params = params - step_rate * (direction + decay_rate * params)
    return (
        output.astype(jnp.bfloat16).reshape(tokens.shape),
        grad_inputs.reshape(tokens.shape),
        grad_shard,
        new_params,
        new_first,
        new_second,
    )


def solution(mesh):
    in_specs = (
        P("dp", "zero", None),
        P("dp", "zero", None),
        P("zero", "dp", None),
        P("zero", "dp", None),
        P("zero", "dp", None),
    )
    out_specs = (
        P("dp", "zero", None),
        P("dp", "zero", None),
        P("zero", "dp", None),
        P("zero", "dp", None),
        P("zero", "dp", None),
        P("zero", "dp", None),
    )
    return jax.shard_map(
        per_device, mesh=mesh, in_specs=in_specs, out_specs=out_specs, check_vma=False
    )
```
